1024 devices in a mesh: grp: 4 (over y_lo, core), lat: 32 (over z), lon: 8 (over x, y_hi).
Axes of the slice: x: 4, y: 4 (y_hi: 2, y_lo: 2; y = y_hi * 2 + y_lo), z: 32, core: 2. Of those that a mesh axis runs over, the one named last changes fastest.
Arguments:
- grid_state: bfloat16 [32, 2560, 5120], P(None, ('grp', 'lat'), 'lon'), may hold values from -6 to 6
- legendre: bfloat16 [128, 1920, 1280], P(('grp', 'lat')), may hold values from -0.125 to 0.125
- sent_field: float32 [2560, 5120], P(('grp', 'lat'), 'lon'), may hold values from -6 to 6
- wet_mask: int32 [2560, 5120], P(('grp', 'lat'), 'lon'), may hold values from 0 to 1, as said below
- diffusivity: float32 [2560, 5120], P(('grp', 'lat'), 'lon'), may hold values from 0.04 to 0.24
- remap_blocks: int32 [128, 8, 8, 3], P(('grp', 'lat'), 'lon'), may hold values from 0 to 99, as said below
- remap_weights: bfloat16 [128, 8, 8, 128, 128], P(('grp', 'lat'), 'lon'), may hold values from -0.5 to 0.5
Outputs:
- spectral: float32 [128, 32, 2, 1280], P(('grp', 'lat'), 'lon')
- received: float32 [2560, 5120], P(('grp', 'lat'), 'lon')
- grid_next: float32 [32, 2560, 5120], P(None, ('grp', 'lat'), 'lon')
The draws below stay inside these ranges and needn't reach their ends.
Inputs may be any that keep to these rules, and one draw needn't show every extreme that they name: wet_mask is 1 on every row below 1920. remap_blocks: field 0 is 3 h + d + 1 with d in -1..1 and h the source group: h = 3 on atmosphere bands, h below 3 on ocean bands; fields 1 and 2 are below 100; entry 0 of every tile names source block 0 and target block 99.
All inputs are finite; a program needn't handle non-finite values.
Results may differ from the reference program's by a relative error of at most 0.0037.
Values may be sent and summed in bfloat16 or wider, within the bound.
No kernel may reach another device: no remote copies, remote signals or barrier semaphores. Data moves between devices by JAX's collectives and lax.ppermute only.
A program may use at most 32 MiB of HBM per device.

```python
import math
import jax
import jax.numpy as jnp
from jax import lax

NLON = 5120
NN = 1280
ROW_DEV = 20
BLK = 128
E_DEV = 8
BANDS = 128
OCEAN_BANDS = 32
ATM_GROUPS = 3
ATM_BANDS = 96
TILES_LON = 8
COL_DEV = 640
ROWS = 2560
NLAT = 1920
FL = 32
MW = 128
TILE_BLOCKS = 100


def draw_wet_mask(key, part):
    levels = jax.random.randint(jax.random.fold_in(key, 29), (ROWS, NLON), 0, 4)
    row_ids = jnp.arange(ROWS, dtype=jnp.int32)[:, None]
    return jnp.where((row_ids < NLAT) | (levels > 0), 1, 0).astype(jnp.int32)


def draw_remap_blocks(key, part):
    keys = jax.random.split(jax.random.fold_in(key, 11), 4)
    shape_all = (BANDS, TILES_LON, E_DEV)
    zeros = jnp.zeros(shape_all, jnp.int32)
    band_ids = jnp.arange(BANDS, dtype=jnp.int32)[:, None, None] + zeros
    entry_ids = jnp.arange(E_DEV, dtype=jnp.int32)[None, None, :] + zeros
    ocean_band = band_ids >= ATM_BANDS
    lon_step = jax.random.randint(keys[0], shape_all, 0, 3)
    source_group = jax.random.randint(keys[1], shape_all, 0, ATM_GROUPS)
    source_group = jnp.where(ocean_band, source_group, ATM_GROUPS)
    neighbour = 3 * source_group + lon_step
    source_ids = jax.random.randint(keys[2], shape_all, 0, TILE_BLOCKS)
    target_ids = jax.random.randint(keys[3], shape_all, 0, TILE_BLOCKS)
    first = entry_ids == 0
    neighbour = jnp.where(first, jnp.where(ocean_band, 0, 3 * ATM_GROUPS + 2), neighbour)
    source_ids = jnp.where(first, 0, source_ids)
    target_ids = jnp.where(first, TILE_BLOCKS - 1, target_ids)
    return jnp.stack([neighbour, source_ids, target_ids], axis=-1).astype(jnp.int32)


def block_levels(rng, extent, cuts, least, largest):
    factor_of = 1.0
    for dim, shards_of in cuts:
        steps = jax.random.uniform(jax.random.fold_in(jax.random.fold_in(rng, 6), dim), (shards_of,), jnp.float32, least / len(cuts), largest / len(cuts))
        factor_of = factor_of * jnp.repeat(jnp.exp(steps), extent[dim] // shards_of).reshape((-1,) + (1,) * (len(extent) - 1 - dim))
    return factor_of


def scatter_about(key, dims, scale, bound, cuts=(), held_as=jnp.bfloat16):
    drawn = jax.random.normal(key, dims, jnp.float32) * scale
    if len(cuts) > 0:
        drawn = block_levels(key, dims, cuts, -0.22, 0.18) * drawn
    return jnp.clip(drawn, min=-bound, max=bound).astype(held_as)


def setup_inputs(seed: int = 0) -> dict:
    seeds = jax.random.split(jax.random.key(seed), 8)
    return {
        "grid_state": scatter_about(seeds[0], (FL, ROWS, NLON), 1.0, 6.0, ((1, 128), (2, 8))),
        "legendre": scatter_about(seeds[1], (MW, NLAT, NN), NLAT ** -0.5, 0.125, ((0, 128),)),
        "sent_field": scatter_about(seeds[2], (ROWS, NLON), 1.0, 6.0, ((0, 128), (1, 8)), jnp.float32),
        "wet_mask": draw_wet_mask(jax.random.fold_in(seeds[7], 71), 0),
        "diffusivity": jnp.clip(jnp.exp(math.log(0.24) - 1.7917595 * jax.random.uniform(seeds[4], (ROWS, NLON), jnp.float32) ** block_levels(seeds[4], (ROWS, NLON), ((0, 128), (1, 8)), -0.2, 0.2)), 0.04, 0.24),
        "remap_blocks": draw_remap_blocks(jax.random.fold_in(seeds[7], 71), 0),
        "remap_weights": scatter_about(seeds[6], (BANDS, TILES_LON, E_DEV, BLK, BLK), BLK ** -0.5, 0.5, ((0, 128), (1, 8))),
    }


def fourier_table(wave_count, lon_first, lon_count, lon_total):
    wave_ids = jnp.arange(wave_count, dtype=jnp.int32)
    longitudes = lon_first + jnp.arange(lon_count, dtype=jnp.int32)
    phases = wave_ids[:, None] * longitudes[None, :] % lon_total
    angles = jnp.float32(2.0 * math.pi / lon_total) * phases.astype(jnp.float32)
    basis_rows = jnp.stack([jnp.cos(angles), -jnp.sin(angles)], axis=1)
    return basis_rows.reshape(2 * wave_count, lon_count).astype(jnp.bfloat16)

def tiles_of(field):
    return field.reshape(BANDS, ROW_DEV, TILES_LON, COL_DEV).transpose(0, 2, 1, 3).reshape(BANDS, TILES_LON, TILE_BLOCKS, BLK)

def field_of(tiles):
    return tiles.reshape(BANDS, TILES_LON, ROW_DEV, COL_DEV).transpose(0, 2, 1, 3).reshape(ROWS, NLON)

def remap_all(listing, weights, source_tiles):
    lon_ids = jnp.arange(TILES_LON, dtype=jnp.int32)[:, None]
    block_ids = jnp.arange(TILE_BLOCKS, dtype=jnp.int32)

    def one_band(inputs):
        band_list, band_weights, band_index = inputs
        source_band = band_list[..., 0] // 3 * OCEAN_BANDS + band_index % OCEAN_BANDS
        source_lon = (lon_ids + band_list[..., 0] % 3 - 1) % TILES_LON
        sources = source_tiles[source_band, source_lon, band_list[..., 1]]
        products = jnp.einsum('leij,lej->lei', band_weights.astype(jnp.float32), sources.astype(jnp.float32), precision=lax.Precision.HIGHEST)
        onehot = (band_list[..., 2][:, None, :] == block_ids[None, :, None]).astype(jnp.float32)
        return jnp.einsum('lte,lei->lti', onehot, products, precision=lax.Precision.HIGHEST)
    return lax.map(one_band, (listing, weights, jnp.arange(BANDS, dtype=jnp.int32)))

def relax(padded_state, padded_wet, diffusion):
    height = padded_state.shape[1] - 2
    breadth = padded_state.shape[2] - 2
    centre = padded_state[:, 1:-1, 1:-1]
    centre_wet = padded_wet[1:-1, 1:-1]
    laplace_sum = jnp.zeros_like(centre)
    for row_shift, col_shift in ((0, 1), (0, -1), (1, 0), (-1, 0)):
        neighbour = padded_state[:, 1 + row_shift:1 + row_shift + height, 1 + col_shift:1 + col_shift + breadth]
        neighbour_wet = padded_wet[1 + row_shift:1 + row_shift + height, 1 + col_shift:1 + col_shift + breadth]
        laplace_sum = laplace_sum + neighbour_wet * (neighbour - centre)
    return centre + diffusion * centre_wet * laplace_sum

def pad_domain(values):
    widths = [(0, 0)] * (values.ndim - 2) + [(1, 1), (1, 1)]
    return jnp.pad(values, widths, mode='wrap')

def two_steps(state, wet_field, diffusion):
    padded_wet = pad_domain(wet_field)
    for repeat in range(2):
        state = relax(pad_domain(state), padded_wet, diffusion)
    return state

def reference(grid_state, legendre, sent_field, wet_mask, diffusivity, remap_blocks, remap_weights):
    basis = fourier_table(MW, 0, NLON, NLON)
    norm_factor = jnp.float32(1.0 / math.sqrt(NLON))

    def one_field(plane):
        summed = jnp.dot(plane, basis.T, preferred_element_type=jnp.float32) * norm_factor
        return summed.astype(jnp.bfloat16)
    fourier = lax.map(one_field, grid_state[:, :NLAT])

    def one_wave(inputs):
        table_rows, wave_index = inputs
        pair = lax.dynamic_slice_in_dim(fourier, (2 * wave_index).astype(jnp.int32), 2, 2)
        pair = pair.transpose(0, 2, 1).reshape(2 * FL, NLAT)
        return jnp.dot(pair, table_rows, preferred_element_type=jnp.float32).reshape(FL, 2, NN)
    spectral = lax.map(one_wave, (legendre, jnp.arange(MW, dtype=jnp.int32)))
    coupled = tiles_of(sent_field.astype(jnp.bfloat16))
    received = field_of(remap_all(remap_blocks, remap_weights, coupled))
    wet_field = wet_mask.astype(jnp.float32)
    forced = grid_state.astype(jnp.float32).at[0].add(wet_field * received)
    grid_next = two_steps(forced, wet_field, diffusivity)
    return (spectral, received, grid_next)
```

```python
import functools
import math

import jax
import jax.numpy as jnp
import numpy as np
from jax import lax
from jax.experimental import pallas as pl
from jax.experimental.pallas import tpu as pltpu
from jax.sharding import PartitionSpec as P

F32 = jnp.float32
BF16 = jnp.bfloat16
I32 = jnp.int32
NT = (((1,), (1,)), ((), ()))
TN = (((0,), (0,)), ((), ()))

ROW_LIST = 40
ROW_EDGE = 48
ROW_WGT = 64
ROW_SENT = 80
SLOT_ROWS = 184
WIDE = 768
EXTRA = 8


def iota(shape, dim):
    return lax.broadcasted_iota(I32, shape, dim)


def onehot(cond):
    return jnp.where(cond, 1.0, 0.0).astype(BF16)


def mm(a, b, dims=(((1,), (0,)), ((), ())), precision=None):
    return lax.dot_general(a, b, dims, preferred_element_type=F32, precision=precision)


def split_hi_lo(x):
    hi = x.astype(BF16).astype(F32)
    return hi, x - hi


def pack_kernel(pos_ref, list_ref, cos_ref, sin_ref, grid_ref, sent_ref, wet_ref, diff_ref, wgt_ref, out_ref):
    me_lon = pos_ref[1]
    turn = (iota((128, 1), 0) * me_lon) & 7
    half = math.sqrt(0.5)

    def eighth(k):
        values = (1.0, half, 0.0, -half, -1.0, -half, 0.0, half)
        out = jnp.zeros((128, 1), F32)
        for i, v in enumerate(values):
            out = jnp.where(((turn + k) & 7) == i, v, out)
        return out

    cos_t, sin_t = eighth(0), eighth(6)
    cos0, sin0 = cos_ref[...], sin_ref[...]
    cos_m = cos_t * cos0 - sin_t * sin0
    sin_m = -(sin_t * cos0 + cos_t * sin0)
    parts = []
    for g in range(4):
        parts += [cos_m[32 * g : 32 * g + 32], sin_m[32 * g : 32 * g + 32]]
    basis = jnp.concatenate(parts, axis=0).astype(BF16)
    state = grid_ref[...].reshape(640, 640)
    sums = mm(state, basis, NT).astype(BF16)
    rho = iota((640, 1), 0)
    jh = (rho >= 320).astype(I32)
    rem = rho - 320 * jh
    tt = (rem * 205) >> 13
    rem = rem - 40 * tt
    j2 = (rem >= 20).astype(I32)
    source = (rem - 20 * j2) * 32 + 4 * tt + 2 * jh + j2
    order = onehot(iota((640, 640), 1) == source)
    moved = mm(order, sums)
    low, high = moved[:320], moved[320:]
    row8, lane8 = iota((8, 128), 0), iota((8, 128), 1)
    listing = jnp.zeros((8, 128), F32)
    for e in range(8):
        for c in range(3):
            listing = jnp.where((row8 == e) & (lane8 == c), list_ref[3 * e + c].astype(F32), listing)
    for g in range(4):
        tile = jnp.concatenate([low[:, 64 * g : 64 * g + 64], high[:, 64 * g : 64 * g + 64]], axis=1)
        for t in range(8):
            block = jnp.concatenate([tile[40 * t : 40 * t + 40], listing], axis=0)
            out_ref[g * 8 + t, 0:48, :] = block.astype(BF16)
    sent = sent_ref[...].astype(BF16)
    pad = jnp.zeros((12, 128), BF16)
    spread = jnp.zeros((104, 128), F32)
    for c in range(5):
        pick = onehot(iota((104, 32), 0) == iota((104, 32), 1) + 20 * c) * onehot(iota((104, 32), 1) < 20)
        spread += mm(pick, jnp.concatenate([sent[:, 128 * c : 128 * c + 128].astype(F32), pad.astype(F32)], axis=0).astype(BF16))
    spread = spread.astype(BF16)
    wet = wet_ref[...].astype(F32)
    dif = diff_ref[...] * wet
    pad12 = jnp.zeros((12, 128), F32)
    edges = []
    for side in range(2):
        base = 0 if side == 0 else 512
        lane0 = 0 if side == 0 else 126
        acc = jnp.zeros((16, 128), F32)
        for k in range(6):
            if k < 5:
                src = grid_ref[4 * k : 4 * k + 4, :, base : base + 128].reshape(128, 128)
            else:
                hi, lo = split_hi_lo(dif[:, base : base + 128])
                src = jnp.concatenate(
                    [wet[:, base : base + 128], pad12, hi, pad12, lo, pad12, jnp.zeros((32, 128), F32)], axis=0
                ).astype(BF16)
            r16, l16 = iota((16, 128), 0), iota((16, 128), 1)
            pick = onehot(((r16 == k) & (l16 == lane0)) | ((r16 == 8 + k) & (l16 == lane0 + 1)))
            acc += mm(pick, src, NT)
        edges.append(acc)
    wgt = []
    for side in range(2):
        pieces = []
        for i in range(2):
            r = i if side == 0 else 126 + i
            rows = jnp.zeros((8, 128), F32)
            for e in range(8):
                rows = jnp.where(row8 == e, wgt_ref[e, (r // 16) * 16 : (r // 16) * 16 + 16, :].astype(F32)[r % 16 : r % 16 + 1], rows)
            pieces.append(rows)
        wgt.append(jnp.concatenate(pieces, axis=0))
    left = jnp.concatenate([edges[0], wgt[0]], axis=0)
    right = jnp.concatenate([edges[1], wgt[1]], axis=0)
    for t in range(8):
        to_left = ((me_lon + 7) & 7) == t
        block = jnp.where(to_left, left, right).astype(BF16)
        for g in range(4):
            out_ref[g * 8 + t, ROW_EDGE:ROW_SENT, :] = block
            out_ref[g * 8 + t, ROW_SENT:SLOT_ROWS, :] = spread


def turn_kernel(recv_ref, out_ref):
    norm = np.float32(1.0 / math.sqrt(5120.0))
    sums = []
    for g in range(3):
        acc = recv_ref[g * 8, 0:48, :].astype(F32)
        for t in range(1, 8):
            acc += recv_ref[g * 8 + t, 0:48, :].astype(F32)
        sums.append(acc[0:40])
    stack = (jnp.concatenate(sums + [jnp.zeros((8, 128), F32)], axis=0) * norm).astype(BF16)
    out = jnp.zeros((256, 128), F32)
    for j2 in range(2):
        lane = iota((128, 128), 0)
        g = (lane >= 20).astype(I32) + (lane >= 40).astype(I32)
        pick = onehot((iota((128, 128), 1) == lane + 20 * g + 20 * j2) & (lane < 60))
        lined = mm(pick, stack).astype(BF16)
        rho, lam = iota((256, 128), 0), iota((256, 128), 1)
        want = ((rho >> 2) & 1) * 64 + (rho & 1) * 32 + (rho >> 3)
        place = onehot((((rho >> 1) & 1) == j2) & (lam == want))
        out += mm(place, lined, NT)
    out_ref[...] = out.astype(BF16)


def remap_kernel(pos_ref, list_ref, recv_ref, wgt_ref, wet_ref, diff_ref, grid_ref,
                 rec_ref, tail_ref, planes_ref, up_ref, down_ref):
    me_grp, me_lon = pos_ref[0], pos_ref[1]
    slot_l = me_grp * 8 + ((me_lon + 7) & 7)
    slot_r = me_grp * 8 + ((me_lon + 1) & 7)
    row8 = iota((8, 1), 0)

    def field(c):
        out = jnp.zeros((8, 1), I32)
        for e in range(8):
            out = jnp.where(row8 == e, list_ref[3 * e + c], out)
        return out

    def ids(k, s, centre):
        h = (k >= 3).astype(I32) + (k >= 6).astype(I32) + (k >= 9).astype(I32)
        lon = (centre + k - 3 * h + 7) & 7
        row = (s * 205) >> 10
        return h * 8 + lon, (s - 5 * row) * 20 + row

    lists = [(field(0), field(1), field(2))]
    for slot in (slot_l, slot_r):
        rows = recv_ref[slot, 32:48, :].astype(F32)[8:16].astype(I32)
        lists.append((rows[:, 0:1], rows[:, 1:2], rows[:, 2:3]))
    pairs = [ids(k, s, me_lon + shift) for (k, s, _), shift in zip(lists, (0, 7, 1))]
    slot_id = jnp.concatenate([p[0] for p in pairs], axis=0)
    block_id = jnp.concatenate([p[1] for p in pairs], axis=0)
    in_block = jnp.where(iota((24, 104), 1) == block_id, 1.0, 0.0)
    source = jnp.zeros((24, 128), F32)
    for slot in range(32):
        pick = jnp.where(slot_id == slot, in_block, 0.0).astype(BF16)
        source += mm(pick, recv_ref[slot, ROW_SENT:SLOT_ROWS, :])
    own = source[0:8].astype(BF16)
    prod = jnp.zeros((8, 128), F32)
    for e in range(8):
        prod = jnp.where(row8 == e, mm(own, wgt_ref[e], NT), prod)
    target = lists[0][2]
    trow = (target * 205) >> 10
    place = jnp.where(iota((8, 256), 1) == (target - 5 * trow) * 32 + trow, 1.0, 0.0)
    placed = mm(place, prod, TN, lax.Precision.HIGHEST)
    tiles = [placed[32 * c : 32 * c + 20] for c in range(5)]
    received = jnp.concatenate(tiles, axis=1)
    rec_ref[...] = received
    lane = iota((8, 128), 1)
    values, spots = [], []
    for n, (slot, lane0, col) in enumerate(((slot_l, 126, 4), (slot_r, 0, 0))):
        rows = recv_ref[slot, ROW_WGT:ROW_SENT, :].astype(F32)
        src = source[8 + 8 * n : 16 + 8 * n]
        v0 = jnp.sum(rows[0:8] * src, axis=1, keepdims=True)
        v1 = jnp.sum(rows[8:16] * src, axis=1, keepdims=True)
        values.append(jnp.where(lane == lane0, v0, 0.0) + jnp.where(lane == lane0 + 1, v1, 0.0))
        goal = lists[1 + n][2]
        grow = (goal * 205) >> 10
        spots.append(jnp.where((iota((8, 128), 1) == grow) & (goal - 5 * grow == col), 1.0, 0.0))
    rec_tail = mm(jnp.concatenate(spots, axis=0), jnp.concatenate(values, axis=0), TN, lax.Precision.HIGHEST)[0:20]
    edge = jnp.concatenate(
        [recv_ref[slot_l, ROW_EDGE:ROW_WGT, :].astype(F32), recv_ref[slot_r, ROW_EDGE:ROW_WGT, :].astype(F32)], axis=0
    ).astype(BF16)
    r32, l32 = iota((32, 128), 0), iota((32, 128), 1)

    def tail_of(k):
        pick = onehot(
            ((r32 == k) & (l32 == 126)) | ((r32 == 8 + k) & (l32 == 127))
            | ((r32 == 16 + k) & (l32 == 0)) | ((r32 == 24 + k) & (l32 == 1))
        )
        return mm(edge, pick, TN)

    for k in range(5):
        tail_ref[4 * k : 4 * k + 4] = tail_of(k).reshape(4, 32, 128).astype(BF16)
    last = tail_of(5)
    wet = jnp.concatenate([wet_ref[...].astype(F32), last[0:20]], axis=1)
    dif = jnp.concatenate([diff_ref[...] * wet_ref[...].astype(F32), last[32:52] + last[64:84]], axis=1)
    force = wet * jnp.concatenate([received, rec_tail], axis=1)
    planes_ref[0] = wet
    planes_ref[1] = dif
    planes_ref[2] = force
    dhi, dlo = split_hi_lo(dif)
    fhi, flo = split_hi_lo(force)
    rowx = iota((EXTRA, WIDE), 0)
    for ref, first in ((up_ref, 0), (down_ref, 18)):
        for i in range(2):
            r = first + i
            ref[i, 0:32, 0:640] = grid_ref[r]
            ref[i, 0:32, 640:WIDE] = tail_ref[r]
            extra = jnp.zeros((EXTRA, WIDE), F32)
            for n, x in enumerate((wet, dhi, dlo, fhi, flo)):
                extra = jnp.where(rowx == n, x[r : r + 1], extra)
            ref[i, 32 : 32 + EXTRA, :] = extra.astype(BF16)


def step_kernel(grid_ref, tail_ref, planes_ref, above_ref, below_ref, out_ref, q_ref, u_ref, wet_ref, dif_ref, c_ref):
    level0 = iota((32, WIDE), 0) == 0

    def load(r, cells, wet, dif, force):
        cells = jnp.where(level0, cells + force, cells)
        wet_ref[r] = jnp.broadcast_to(wet, (8, WIDE))
        dif_ref[r] = jnp.broadcast_to(dif, (8, WIDE))
        q_ref[r] = cells
        u_ref[r] = cells * wet

    for i in range(2):
        for ref, r in ((above_ref, i), (below_ref, 22 + i)):
            extra = ref[i, 32 : 32 + EXTRA, :].astype(F32) if EXTRA == 16 else ref[i, 32:40, :].astype(F32)
            load(r, ref[i, 0:32, :].astype(F32), extra[0:1], extra[1:2] + extra[2:3], extra[3:4] + extra[4:5])
    for r in range(20):
        cells = jnp.concatenate([grid_ref[r].astype(F32), tail_ref[r].astype(F32)], axis=1)
        load(r + 2, cells, planes_ref[0, r : r + 1, :], planes_ref[1, r : r + 1, :], planes_ref[2, r : r + 1, :])

    def sides(x):
        return pltpu.roll(x, 1, axis=1) + pltpu.roll(x, WIDE - 1, axis=1)

    def coef(r, carry):
        near = wet_ref[r - 1] + wet_ref[r + 1] + sides(wet_ref[r])
        c_ref[r] = 1.0 - dif_ref[r] * near
        return carry

    lax.fori_loop(1, 23, coef, 0)

    def four(x):
        return jnp.concatenate([x] * 4, axis=0)

    def first(r, prev):
        here = u_ref[r]
        total = sides(here) + prev + u_ref[r + 1]
        q = q_ref[r] * four(c_ref[r]) + four(dif_ref[r]) * total
        q_ref[r] = q
        u_ref[r] = q * four(wet_ref[r])
        return here

    lax.fori_loop(1, 23, first, u_ref[0])

    def second(r, carry):
        total = sides(u_ref[r]) + u_ref[r - 1] + u_ref[r + 1]
        q = q_ref[r] * four(c_ref[r]) + four(dif_ref[r]) * total
        out_ref[r - 2] = q[:, 0:640]
        return carry

    lax.fori_loop(2, 22, second, 0)


VMEM = pl.BlockSpec(memory_space=pltpu.VMEM)
SMEM = pl.BlockSpec(memory_space=pltpu.SMEM)
PARAMS = pltpu.CompilerParams(vmem_limit_bytes=40 * 1024 * 1024)


def call(kernel, name, smem, vmem, outs, scratch=()):
    flat = [jax.ShapeDtypeStruct(s, d) for s, d in outs]
    return pl.pallas_call(
        kernel,
        name=name,
        out_shape=flat if len(flat) > 1 else flat[0],
        in_specs=[SMEM] * len(smem) + [VMEM] * len(vmem),
        out_specs=[VMEM] * len(flat) if len(flat) > 1 else VMEM,
        scratch_shapes=list(scratch),
        compiler_params=PARAMS,
    )(*smem, *vmem)


def trig_tables():
    phase = np.arange(128)[:, None] * np.arange(640)[None, :] % 5120
    angle = 2.0 * np.pi / 5120.0 * phase
    return np.cos(angle).astype(np.float32), np.sin(angle).astype(np.float32)


def shards(grid_state, legendre, sent_field, wet_mask, diffusivity, remap_blocks, remap_weights):
    rows = grid_state.transpose(1, 0, 2)
    pos = jnp.stack([lax.axis_index("grp"), lax.axis_index("lon")]).astype(I32)
    listing = remap_blocks.reshape(24)
    weights = remap_weights[0, 0]
    cos0, sin0 = trig_tables()
    packed = call(
        pack_kernel, "pack", (pos, listing),
        (jnp.asarray(cos0), jnp.asarray(sin0), rows, sent_field, wet_mask, diffusivity, weights),
        [((32, SLOT_ROWS, 128), BF16)],
    )
    plane = lax.all_to_all(packed, ("grp", "lon"), 0, 0, tiled=True)
    turned = call(turn_kernel, "turn", (), (plane,), [((256, 128), BF16)])
    waves = lax.all_to_all(turned.reshape(32, 8, 128), "lat", 0, 0, tiled=True)
    received, tail, planes, up, down = call(
        remap_kernel, "remap", (pos, listing), (plane, weights, wet_mask, diffusivity, rows),
        [((20, 640), F32), ((20, 32, 128), BF16), ((3, 20, WIDE), F32),
         ((2, 32 + EXTRA, WIDE), BF16), ((2, 32 + EXTRA, WIDE), BF16)],
    )
    bands = lax.axis_size(("grp", "lat"))
    below = lax.ppermute(up, ("grp", "lat"), [((i + 1) % bands, i) for i in range(bands)])
    above = lax.ppermute(down, ("grp", "lat"), [(i, (i + 1) % bands) for i in range(bands)])
    stepped = call(
        step_kernel, "step", (), (rows, tail, planes, above, below),
        [((20, 32, 640), F32)],
        scratch=[pltpu.VMEM((24, 32, WIDE), F32), pltpu.VMEM((24, 32, WIDE), F32),
                 pltpu.VMEM((24, 8, WIDE), F32), pltpu.VMEM((24, 8, WIDE), F32), pltpu.VMEM((24, 8, WIDE), F32)],
    )
    grid_next = stepped.transpose(1, 0, 2)
    left = waves[:, :, :60].reshape(32, 8, 3, 20).transpose(1, 2, 0, 3).reshape(8, 1920)
    spectral = mm(left, legendre[0]).reshape(1, 4, 2, 1280)
    return spectral, received, grid_next


def solution(mesh):
    in_specs = (
        P(None, ("grp", "lat"), "lon"),
        P(("grp", "lat"), None, None),
        P(("grp", "lat"), "lon"),
        P(("grp", "lat"), "lon"),
        P(("grp", "lat"), "lon"),
        P(("grp", "lat"), "lon", None, None),
        P(("grp", "lat"), "lon", None, None, None),
    )
    out_specs = (
        P(("grp", "lat"), "lon", None, None),
        P(("grp", "lat"), "lon"),
        P(None, ("grp", "lat"), "lon"),
    )
    return jax.shard_map(shards, mesh=mesh, in_specs=in_specs, out_specs=out_specs, check_vma=False)
```

```python
import functools
import math

import jax
import jax.numpy as jnp
import numpy as np
from jax import lax
from jax.experimental import pallas as pl
from jax.experimental.pallas import tpu as pltpu
from jax.sharding import PartitionSpec as P

F32 = jnp.float32
BF16 = jnp.bfloat16
I32 = jnp.int32
NT = (((1,), (1,)), ((), ()))
TN = (((0,), (0,)), ((), ()))

WIDE = 768
ROW_EDGE = 48
ROW_WGT = 64
ROW_SENT = 80
SLOT_ROWS = 184


def iota(shape, dim):
    return lax.broadcasted_iota(I32, shape, dim)


def onehot(cond):
    return jnp.where(cond, 1.0, 0.0).astype(BF16)


def mm(a, b, dims=(((1,), (0,)), ((), ())), precision=None):
    return lax.dot_general(a, b, dims, preferred_element_type=F32, precision=precision)


def upright(x):
    return jnp.sum(jnp.where(iota((8, 8), 0) == iota((8, 8), 1), x, 0), axis=1, keepdims=True)


def split_hi_lo(x):
    hi = x.astype(BF16).astype(F32)
    return hi, x - hi


def pack_kernel(cos_hbm, sin_hbm, list_hbm, grid_hbm, sent_hbm, wet_hbm, diff_hbm, wgt_hbm,
                out_ref, cos_ref, sin_ref, list_ref, grid_ref, sent_ref, wet_ref, diff_ref, wgt_ref, sems):
    pairs = [(cos_hbm, cos_ref), (sin_hbm, sin_ref), (list_hbm, list_ref), (grid_hbm, grid_ref), (sent_hbm, sent_ref),
             (wet_hbm, wet_ref), (diff_hbm, diff_ref)]
    pairs += [(wgt_hbm.at[:, pl.ds(112 * side, 16), :], wgt_ref.at[side]) for side in range(2)]
    copies = [pltpu.make_async_copy(a, b, sems.at[i]) for i, (a, b) in enumerate(pairs)]
    for c in copies:
        c.start()
    me_lon = lax.axis_index("lon")
    turn = (iota((128, 1), 0) * me_lon) & 7
    half = math.sqrt(0.5)

    def eighth(k):
        values = (1.0, half, 0.0, -half, -1.0, -half, 0.0, half)
        out = jnp.zeros((128, 1), F32)
        for i, v in enumerate(values):
            out = jnp.where(((turn + k) & 7) == i, v, out)
        return out

    cos_t, sin_t = eighth(0), eighth(6)
    rho = iota((640, 1), 0)
    jh = (rho >= 320).astype(I32)
    rem = rho - 320 * jh
    tt = (rem * 205) >> 13
    rem = rem - 40 * tt
    j2 = (rem >= 20).astype(I32)
    source = (rem - 20 * j2) * 32 + 4 * tt + 2 * jh + j2
    order = onehot(iota((640, 640), 1) == source)
    row8, lane8 = iota((8, 128), 0), iota((8, 128), 1)
    for c in copies[:3]:
        c.wait()
    listing = jnp.zeros((8, 128), F32)
    for c in range(3):
        listing = jnp.where(lane8 == c, upright(list_ref[c]).astype(F32), listing)
    cos0, sin0 = cos_ref[...], sin_ref[...]
    cos_m = cos_t * cos0 - sin_t * sin0
    sin_m = -(sin_t * cos0 + cos_t * sin0)
    parts = []
    for g in range(4):
        parts += [cos_m[32 * g : 32 * g + 32], sin_m[32 * g : 32 * g + 32]]
    basis = jnp.concatenate(parts, axis=0).astype(BF16)
    for c in copies[3:]:
        c.wait()
    sums = mm(grid_ref[...].reshape(640, 640), basis, NT).astype(BF16)
    moved = mm(order, sums)
    low, high = moved[:320], moved[320:]
    for g in range(4):
        tile = jnp.concatenate([low[:, 64 * g : 64 * g + 64], high[:, 64 * g : 64 * g + 64]], axis=1)
        for t in range(8):
            block = jnp.concatenate([tile[40 * t : 40 * t + 40], listing], axis=0)
            out_ref[g * 8 + t, 0:ROW_EDGE, :] = block.astype(BF16)
    sent = sent_ref[...]
    spread = jnp.zeros((104, 128), F32)
    for c in range(5):
        pick = onehot((iota((104, 32), 0) == iota((104, 32), 1) + 20 * c) & (iota((104, 32), 1) < 20))
        block = jnp.concatenate([sent[:, 128 * c : 128 * c + 128], jnp.zeros((12, 128), F32)], axis=0)
        spread += mm(pick, block.astype(BF16))
    spread = spread.astype(BF16)
    wet = wet_ref[...].astype(F32)
    dif = diff_ref[...] * wet
    pad = jnp.zeros((12, 128), F32)
    blocks = []
    for side in range(2):
        base, lane0 = 512 * side, 126 * side
        edge = jnp.zeros((16, 128), F32)
        for k in range(6):
            if k < 5:
                src = grid_ref[4 * k : 4 * k + 4, :, base : base + 128].reshape(128, 128)
            else:
                hi, lo = split_hi_lo(dif[:, base : base + 128])
                src = jnp.concatenate(
                    [wet[:, base : base + 128], pad, hi, pad, lo, pad, jnp.zeros((32, 128), F32)], axis=0
                ).astype(BF16)
            r16, l16 = iota((16, 128), 0), iota((16, 128), 1)
            pick = onehot(((r16 == k) & (l16 == lane0)) | ((r16 == 8 + k) & (l16 == lane0 + 1)))
            edge += mm(pick, src, NT)
        pieces = [edge]
        for i in range(2):
            rows = jnp.zeros((8, 128), F32)
            for e in range(8):
                rows = jnp.where(row8 == e, wgt_ref[side, e].astype(F32)[14 * side + i : 14 * side + i + 1], rows)
            pieces.append(rows)
        blocks.append(jnp.concatenate(pieces, axis=0))
    for t in range(8):
        to_left = ((me_lon + 7) & 7) == t
        block = jnp.where(to_left, blocks[0], blocks[1]).astype(BF16)
        for g in range(4):
            out_ref[g * 8 + t, ROW_EDGE:ROW_SENT, :] = block
            out_ref[g * 8 + t, ROW_SENT:SLOT_ROWS, :] = spread


def rim_kernel(wet_hbm, diff_hbm, grid_hbm, up_ref, down_ref, wet_ref, diff_ref, rows_ref, sems):
    pairs = [(wet_hbm, wet_ref), (diff_hbm, diff_ref), (grid_hbm.at[0:2], rows_ref.at[0:2]),
             (grid_hbm.at[18:20], rows_ref.at[2:4])]
    copies = [pltpu.make_async_copy(a, b, sems.at[i]) for i, (a, b) in enumerate(pairs)]
    for c in copies:
        c.start()
    for c in copies:
        c.wait()
    row8 = iota((8, 640), 0)
    for n, (ref, first) in enumerate(((up_ref, 0), (down_ref, 18))):
        for i in range(2):
            r = first + i
            wet = wet_ref[r : r + 1, :].astype(F32)
            hi, lo = split_hi_lo(diff_ref[r : r + 1, :] * wet)
            extra = jnp.zeros((8, 640), F32)
            for m, x in enumerate((wet, hi, lo)):
                extra = jnp.where(row8 == m, x, extra)
            ref[i, 0:32, :] = rows_ref[2 * n + i]
            ref[i, 32:40, :] = extra.astype(BF16)


def remap_kernel(list_ref, recv_ref, wgt_ref, wet_ref, diff_ref,
                 rec_ref, tail_ref, planes_ref, up_ref, down_ref):
    me_grp, me_lon = lax.axis_index("grp"), lax.axis_index("lon")
    slot_l = me_grp * 8 + ((me_lon + 7) & 7)
    slot_r = me_grp * 8 + ((me_lon + 1) & 7)
    row8 = iota((8, 1), 0)

    def ids(k, s, centre):
        h = (k >= 3).astype(I32) + (k >= 6).astype(I32) + (k >= 9).astype(I32)
        lon = (centre + k - 3 * h + 7) & 7
        row = (s * 205) >> 10
        return h * 8 + lon, (s - 5 * row) * 20 + row

    lists = [tuple(upright(list_ref[c]) for c in range(3))]
    for slot in (slot_l, slot_r):
        rows = recv_ref[slot, 32:48, :].astype(F32)[8:16].astype(I32)
        lists.append((rows[:, 0:1], rows[:, 1:2], rows[:, 2:3]))
    pairs = [ids(k, s, me_lon + shift) for (k, s, _), shift in zip(lists, (0, 7, 1))]
    slot_id = jnp.concatenate([p[0] for p in pairs], axis=0)
    block_id = jnp.concatenate([p[1] for p in pairs], axis=0)
    in_block = jnp.where(iota((24, 104), 1) == block_id, 1.0, 0.0)
    source = jnp.zeros((24, 128), F32)
    for slot in range(32):
        pick = jnp.where(slot_id == slot, in_block, 0.0).astype(BF16)
        source += mm(pick, recv_ref[slot, ROW_SENT:SLOT_ROWS, :])
    own = source[0:8].astype(BF16)
    prod = jnp.zeros((8, 128), F32)
    for e in range(8):
        prod = jnp.where(row8 == e, mm(own, wgt_ref[e], NT), prod)
    target = lists[0][2]
    trow = (target * 205) >> 10
    place = jnp.where(iota((8, 256), 1) == (target - 5 * trow) * 32 + trow, 1.0, 0.0)
    placed = mm(place, prod, TN, lax.Precision.HIGHEST)
    received = jnp.concatenate([placed[32 * c : 32 * c + 20] for c in range(5)], axis=1)
    rec_ref[...] = received
    lane = iota((8, 128), 1)
    values, spots = [], []
    for n, (slot, lane0, col) in enumerate(((slot_l, 126, 4), (slot_r, 0, 0))):
        rows = recv_ref[slot, ROW_WGT:ROW_SENT, :].astype(F32)
        src = source[8 + 8 * n : 16 + 8 * n]
        v0 = jnp.sum(rows[0:8] * src, axis=1, keepdims=True)
        v1 = jnp.sum(rows[8:16] * src, axis=1, keepdims=True)
        values.append(jnp.where(lane == lane0, v0, 0.0) + jnp.where(lane == lane0 + 1, v1, 0.0))
        goal = lists[1 + n][2]
        grow = (goal * 205) >> 10
        spots.append(jnp.where((lane == grow) & (goal - 5 * grow == col), 1.0, 0.0))
    rec_tail = mm(jnp.concatenate(spots, axis=0), jnp.concatenate(values, axis=0), TN, lax.Precision.HIGHEST)[0:20]
    edge = jnp.concatenate(
        [recv_ref[slot_l, ROW_EDGE:ROW_WGT, :].astype(F32), recv_ref[slot_r, ROW_EDGE:ROW_WGT, :].astype(F32)], axis=0
    ).astype(BF16)
    r32, l32 = iota((32, 128), 0), iota((32, 128), 1)

    def tail_of(k):
        pick = onehot(
            ((r32 == k) & (l32 == 126)) | ((r32 == 8 + k) & (l32 == 127))
            | ((r32 == 16 + k) & (l32 == 0)) | ((r32 == 24 + k) & (l32 == 1))
        )
        return mm(edge, pick, TN)

    for k in range(5):
        tail_ref[4 * k : 4 * k + 4] = tail_of(k).reshape(4, 32, 128).astype(BF16)
    last = tail_of(5)
    own_wet = wet_ref[...].astype(F32)
    wet = jnp.concatenate([own_wet, last[0:20]], axis=1)
    dif = jnp.concatenate([diff_ref[...] * own_wet, last[32:52] + last[64:84]], axis=1)
    force = wet * jnp.concatenate([received, rec_tail], axis=1)
    planes_ref[0] = wet
    planes_ref[1] = dif
    planes_ref[2] = force
    fhi, flo = split_hi_lo(force)
    row16 = iota((16, 128), 0)
    for ref, first in ((up_ref, 0), (down_ref, 18)):
        for i in range(2):
            r = first + i
            ref[i, 0:32, :] = tail_ref[r]
            extra = jnp.zeros((16, 128), F32)
            lines = [x[r : r + 1, 128 * c : 128 * c + 128] for x in (fhi, flo) for c in range(6)]
            lines += [last[r : r + 1], last[32 + r : 33 + r], last[64 + r : 65 + r]]
            for m, x in enumerate(lines):
                extra = jnp.where(row16 == m, x, extra)
            ref[i, 32:48, :] = extra.astype(BF16)


def step_kernel(tail_ref, planes_ref, above_ref, below_ref, above2_ref, below2_ref, grid_ref,
                out_hbm, q_ref, u_ref, q1_ref, u1_ref, wet_ref, dif_ref, c_ref, res_ref, sems):
    level0 = iota((8, WIDE), 0) == 0

    def load(r, row, end, wet, dif, force):
        wet = jnp.broadcast_to(wet, (8, WIDE))
        wet_ref[r] = wet
        dif_ref[r] = jnp.broadcast_to(dif, (8, WIDE))
        cells = jnp.concatenate([row.astype(F32), end.astype(F32)], axis=1)
        for v in range(4):
            part = cells[8 * v : 8 * v + 8]
            if v == 0:
                part = jnp.where(level0, part + force, part)
            q_ref[r, 8 * v : 8 * v + 8, :] = part
            u_ref[r, 8 * v : 8 * v + 8, :] = part * wet

    for ref, ref2, base in ((above_ref, above2_ref, 0), (below_ref, below2_ref, 22)):
        for i in range(2):
            near = ref[i, 32:40, :].astype(F32)
            far = ref2[i, 32:48, :].astype(F32)
            wet = jnp.concatenate([near[0:1], far[12:13]], axis=1)
            dif = jnp.concatenate([near[1:2] + near[2:3], far[13:14] + far[14:15]], axis=1)
            force = jnp.concatenate([far[c : c + 1] + far[6 + c : 7 + c] for c in range(6)], axis=1)
            load(base + i, ref[i, 0:32, :], ref2[i, 0:32, :], wet, dif, force)
    for r in range(20):
        load(r + 2, grid_ref[r], tail_ref[r], planes_ref[0, r : r + 1, :], planes_ref[1, r : r + 1, :],
             planes_ref[2, r : r + 1, :])

    def sides(x):
        return pltpu.roll(x, 1, axis=1) + pltpu.roll(x, WIDE - 1, axis=1)

    def first(r, carry):
        dif = dif_ref[r]
        wet = wet_ref[r]
        coef = 1.0 - dif * (wet_ref[r - 1] + wet_ref[r + 1] + sides(wet))
        c_ref[r] = coef
        for v in range(4):
            lev = pl.ds(8 * v, 8)
            total = sides(u_ref[r, lev, :]) + u_ref[r - 1, lev, :] + u_ref[r + 1, lev, :]
            q = q_ref[r, lev, :] * coef + dif * total
            q1_ref[r, lev, :] = q
            u1_ref[r, lev, :] = q * wet
        return carry

    lax.fori_loop(1, 23, first, 0)

    def copy(r):
        return pltpu.make_async_copy(res_ref.at[r], out_hbm.at[r], sems.at[r])

    def second(r, carry):
        coef = c_ref[r]
        dif = dif_ref[r]
        for v in range(4):
            lev = pl.ds(8 * v, 8)
            total = sides(u1_ref[r, lev, :]) + u1_ref[r - 1, lev, :] + u1_ref[r + 1, lev, :]
            q = q1_ref[r, lev, :] * coef + dif * total
            res_ref[r - 2, lev, :] = q[:, 0:640]
        copy(r - 2).start()
        return carry

    lax.fori_loop(2, 22, second, 0)

    def finish(r, carry):
        copy(r).wait()
        return carry

    lax.fori_loop(0, 20, finish, 0)


def turn_kernel(recv_ref, out_ref):
    norm = np.float32(1.0 / math.sqrt(5120.0))
    sums = []
    for g in range(3):
        acc = recv_ref[g * 8, 0:48, :].astype(F32)
        for t in range(1, 8):
            acc += recv_ref[g * 8 + t, 0:48, :].astype(F32)
        sums.append(acc[0:40])
    stack = (jnp.concatenate(sums + [jnp.zeros((8, 128), F32)], axis=0) * norm).astype(BF16)
    out = jnp.zeros((256, 128), F32)
    for j2 in range(2):
        lane = iota((128, 128), 0)
        g = (lane >= 20).astype(I32) + (lane >= 40).astype(I32)
        pick = onehot((iota((128, 128), 1) == lane + 20 * g + 20 * j2) & (lane < 60))
        lined = mm(pick, stack).astype(BF16)
        rho, lam = iota((256, 128), 0), iota((256, 128), 1)
        want = ((rho >> 2) & 1) * 64 + (rho & 1) * 32 + (rho >> 3)
        place = onehot((((rho >> 1) & 1) == j2) & (lam == want))
        out += mm(place, lined, NT)
    out_ref[...] = out.astype(BF16)


def legendre_kernel(waves_hbm, table_hbm, after_hbm, out_ref, waves_ref, table_ref, sems):
    copies = [
        pltpu.make_async_copy(table_hbm.at[pl.ds(128 * i, 128), :], table_ref.at[pl.ds(128 * i, 128), :], sems.at[i])
        for i in range(15)
    ]
    first = pltpu.make_async_copy(waves_hbm, waves_ref, sems.at[15])
    first.start()
    for c in copies:
        c.start()
    first.wait()
    lane = iota((8, 128), 1)
    waves = [waves_ref[l].astype(F32) for l in range(32)]
    tiles = []
    for tau in range(15):
        tile = jnp.zeros((8, 128), F32)
        for g in range(3):
            for l in range(32):
                start = g * 640 + l * 20 - 128 * tau
                if start <= -20 or start >= 128:
                    continue
                shift = (start - 20 * g) % 128
                moved = pltpu.roll(waves[l], shift, axis=1) if shift else waves[l]
                tile = jnp.where((lane >= start) & (lane < start + 20), moved, tile)
        tiles.append(tile)
    out = jnp.zeros((8, 1280), F32)
    for i in range(15):
        copies[i].wait()
        out += mm(tiles[i].astype(BF16), table_ref[128 * i : 128 * i + 128, :])
    for j in range(4):
        out_ref[j] = out[2 * j : 2 * j + 2]


VMEM = pl.BlockSpec(memory_space=pltpu.VMEM)
SMEM = pl.BlockSpec(memory_space=pltpu.SMEM)
HBM = pl.BlockSpec(memory_space=pltpu.HBM)


def call(kernel, name, smem, vmem, hbm, outs, scratch=(), out_space=VMEM, limit=None):
    flat = [jax.ShapeDtypeStruct(s, d) for s, d in outs]
    return pl.pallas_call(
        kernel,
        name=name,
        out_shape=flat if len(flat) > 1 else flat[0],
        in_specs=[SMEM] * len(smem) + [VMEM] * len(vmem) + [HBM] * len(hbm),
        out_specs=[out_space] * len(flat) if len(flat) > 1 else out_space,
        scratch_shapes=list(scratch),
        compiler_params=pltpu.CompilerParams(vmem_limit_bytes=limit and limit * 1024 * 1024),
    )(*smem, *vmem, *hbm)


def trig_tables():
    phase = np.arange(128)[:, None] * np.arange(640)[None, :] % 5120
    angle = 2.0 * np.pi / 5120.0 * phase
    return np.cos(angle).astype(np.float32), np.sin(angle).astype(np.float32)


def shards(grid_state, legendre, sent_field, wet_mask, diffusivity, remap_blocks, remap_weights):
    rows = grid_state.transpose(1, 0, 2)
    listing = remap_blocks.transpose(0, 3, 1, 2).reshape(3, 1, 8)
    weights = remap_weights[0, 0]
    bands = lax.axis_size(("grp", "lat"))
    to_before = [((i + 1) % bands, i) for i in range(bands)]
    to_after = [(i, (i + 1) % bands) for i in range(bands)]
    cos0, sin0 = trig_tables()
    packed = call(
        pack_kernel, "pack", (), (),
        (jnp.asarray(cos0), jnp.asarray(sin0), listing, rows, sent_field, wet_mask, diffusivity, weights),
        [((32, SLOT_ROWS, 128), BF16)],
        scratch=[pltpu.VMEM((128, 640), F32), pltpu.VMEM((128, 640), F32), pltpu.VMEM((3, 1, 8), I32), pltpu.VMEM((20, 32, 640), BF16),
                 pltpu.VMEM((20, 640), F32), pltpu.VMEM((20, 640), I32), pltpu.VMEM((20, 640), F32),
                 pltpu.VMEM((2, 8, 16, 128), BF16), pltpu.SemaphoreType.DMA((9,))],
    )
    plane = lax.all_to_all(packed, ("grp", "lon"), 0, 0, tiled=True)
    up, down = call(
        rim_kernel, "rim", (), (), (wet_mask, diffusivity, rows),
        [((2, 40, 640), BF16), ((2, 40, 640), BF16)],
        scratch=[pltpu.VMEM((20, 640), I32), pltpu.VMEM((20, 640), F32), pltpu.VMEM((4, 32, 640), BF16),
                 pltpu.SemaphoreType.DMA((4,))],
    )
    below = lax.ppermute(up, ("grp", "lat"), to_before)
    above = lax.ppermute(down, ("grp", "lat"), to_after)
    plane, above, below = lax.optimization_barrier((plane, above, below))
    turned = call(turn_kernel, "turn", (), (plane,), (), [((256, 128), BF16)], limit=16)
    waves = lax.all_to_all(turned.reshape(32, 8, 128), "lat", 0, 0, tiled=True)
    received, tail, planes, up2, down2 = call(
        remap_kernel, "remap", (), (listing, plane, weights, wet_mask, diffusivity), (),
        [((20, 640), F32), ((20, 32, 128), BF16), ((3, 20, WIDE), F32), ((2, 48, 128), BF16), ((2, 48, 128), BF16)],
        limit=16,
    )
    below2 = lax.ppermute(up2, ("grp", "lat"), to_before)
    above2 = lax.ppermute(down2, ("grp", "lat"), to_after)
    stepped = call(
        step_kernel, "step", (), (tail, planes, above, below, above2, below2, rows), (),
        [((20, 32, 640), F32)],
        scratch=[pltpu.VMEM((24, 32, WIDE), F32)] * 4 + [pltpu.VMEM((24, 8, WIDE), F32)] * 3
        + [pltpu.VMEM((20, 32, 640), F32), pltpu.SemaphoreType.DMA((20,))],
        out_space=HBM, limit=32,
    )
    spectral = call(
        legendre_kernel, "legendre", (), (), (waves, legendre[0], stepped), [((4, 2, 1280), F32)],
        scratch=[pltpu.VMEM((32, 8, 128), BF16), pltpu.VMEM((1920, 1280), BF16), pltpu.SemaphoreType.DMA((16,))],
    )
    return spectral.reshape(1, 4, 2, 1280), received, stepped.transpose(1, 0, 2)


def solution(mesh):
    in_specs = (
        P(None, ("grp", "lat"), "lon"),
        P(("grp", "lat"), None, None),
        P(("grp", "lat"), "lon"),
        P(("grp", "lat"), "lon"),
        P(("grp", "lat"), "lon"),
        P(("grp", "lat"), "lon", None, None),
        P(("grp", "lat"), "lon", None, None, None),
    )
    out_specs = (
        P(("grp", "lat"), "lon", None, None),
        P(("grp", "lat"), "lon"),
        P(None, ("grp", "lat"), "lon"),
    )
    return jax.shard_map(shards, mesh=mesh, in_specs=in_specs, out_specs=out_specs, check_vma=False)
```

```python
import functools
import math

import jax
import jax.numpy as jnp
import numpy as np
from jax import lax
from jax.experimental import pallas as pl
from jax.experimental.pallas import tpu as pltpu
from jax.sharding import PartitionSpec as P

F32 = jnp.float32
BF16 = jnp.bfloat16
I32 = jnp.int32
NT = (((1,), (1,)), ((), ()))
TN = (((0,), (0,)), ((), ()))

WIDE = 768
ROW_WGT = 16
ROW_LIST = 32
AREA = 104
SLOT_ROWS = 144


def iota(shape, dim):
    return lax.broadcasted_iota(I32, shape, dim)


def onehot(cond):
    return jnp.where(cond, 1.0, 0.0).astype(BF16)


def mm(a, b, dims=(((1,), (0,)), ((), ())), precision=None):
    return lax.dot_general(a, b, dims, preferred_element_type=F32, precision=precision)


def upright(x):
    return jnp.sum(jnp.where(iota((8, 8), 0) == iota((8, 8), 1), x, 0), axis=1, keepdims=True)


def split_hi_lo(x):
    hi = x.astype(BF16).astype(F32)
    return hi, x - hi


def pack_kernel(cos_hbm, sin_hbm, list_hbm, grid_hbm, sent_hbm, wet_hbm, diff_hbm, wgt_hbm,
                out_ref, cos_ref, sin_ref, list_ref, grid_ref, sent_ref, wet_ref, diff_ref, wgt_ref, sems):
    pairs = [(list_hbm, list_ref), (sent_hbm, sent_ref), (wet_hbm, wet_ref), (diff_hbm, diff_ref)]
    pairs += [(wgt_hbm.at[:, pl.ds(112 * side, 16), :], wgt_ref.at[side]) for side in range(2)]
    pairs += [(cos_hbm, cos_ref), (sin_hbm, sin_ref), (grid_hbm, grid_ref)]
    copies = [pltpu.make_async_copy(a, b, sems.at[i]) for i, (a, b) in enumerate(pairs)]
    for c in copies:
        c.start()
    me_lon = lax.axis_index("lon")
    turn = (iota((128, 1), 0) * me_lon) & 7
    half = math.sqrt(0.5)

    def eighth(k):
        values = (1.0, half, 0.0, -half, -1.0, -half, 0.0, half)
        out = jnp.zeros((128, 1), F32)
        for i, v in enumerate(values):
            out = jnp.where(((turn + k) & 7) == i, v, out)
        return out

    cos_t, sin_t = eighth(0), eighth(6)
    rho = iota((640, 1), 0)
    jh = (rho >= 320).astype(I32)
    rem = rho - 320 * jh
    tt = (rem * 205) >> 13
    rem = rem - 40 * tt
    j2 = (rem >= 20).astype(I32)
    source = (rem - 20 * j2) * 32 + 4 * tt + 2 * jh + j2
    order = onehot(iota((640, 640), 1) == source)
    row8, lane8 = iota((8, 128), 0), iota((8, 128), 1)
    for c in copies[:6]:
        c.wait()
    listing = jnp.zeros((8, 128), F32)
    for c in range(3):
        listing = jnp.where(lane8 == c, upright(list_ref[c]).astype(F32), listing)
    sent = sent_ref[...]
    spread = jnp.zeros((104, 128), F32)
    for c in range(5):
        pick = onehot((iota((104, 32), 0) == iota((104, 32), 1) + 20 * c) & (iota((104, 32), 1) < 20))
        block = jnp.concatenate([sent[:, 128 * c : 128 * c + 128], jnp.zeros((12, 128), F32)], axis=0)
        spread += mm(pick, block.astype(BF16))
    wet = wet_ref[...].astype(F32)
    dif = diff_ref[...] * wet
    pad = jnp.zeros((12, 128), F32)
    wgt, planes = [], []
    for side in range(2):
        base = 512 * side
        hi, lo = split_hi_lo(dif[:, base : base + 128])
        planes.append(jnp.concatenate(
            [wet[:, base : base + 128], pad, hi, pad, lo, pad, jnp.zeros((32, 128), F32)], axis=0
        ).astype(BF16))
        for i in range(2):
            rows = jnp.zeros((8, 128), F32)
            for e in range(8):
                rows = jnp.where(row8 == e, wgt_ref[side, e].astype(F32)[14 * side + i : 14 * side + i + 1], rows)
            wgt.append(rows)
    for c in copies[6:8]:
        c.wait()
    cos0, sin0 = cos_ref[...], sin_ref[...]
    cos_m = cos_t * cos0 - sin_t * sin0
    sin_m = -(sin_t * cos0 + cos_t * sin0)
    parts = []
    for g in range(4):
        parts += [cos_m[32 * g : 32 * g + 32], sin_m[32 * g : 32 * g + 32]]
    basis = jnp.concatenate(parts, axis=0).astype(BF16)
    copies[8].wait()
    sums = mm(grid_ref[...].reshape(640, 640), basis, NT).astype(BF16)
    blocks = []
    for side in range(2):
        base, lane0 = 512 * side, 126 * side
        edge = jnp.zeros((16, 128), F32)
        for k in range(6):
            src = grid_ref[4 * k : 4 * k + 4, :, base : base + 128].reshape(128, 128) if k < 5 else planes[side]
            r16, l16 = iota((16, 128), 0), iota((16, 128), 1)
            pick = onehot(((r16 == k) & (l16 == lane0)) | ((r16 == 8 + k) & (l16 == lane0 + 1)))
            edge += mm(pick, src, NT)
        pieces = [edge, wgt[2 * side], wgt[2 * side + 1], listing, jnp.zeros((AREA - 40, 128), F32)]
        blocks.append(jnp.concatenate(pieces, axis=0))
    for g in range(4):
        same = lax.axis_index("grp") == g
        left = jnp.where(same, blocks[0], spread)
        right = jnp.where(same, blocks[1], spread)
        for t in range(8):
            to_left = ((me_lon + 7) & 7) == t
            out_ref[g * 8 + t, 0:AREA, :] = jnp.where(to_left, left, right).astype(BF16)
    moved = mm(order, sums)
    low, high = moved[:320], moved[320:]
    for g in range(4):
        tile = jnp.concatenate([low[:, 64 * g : 64 * g + 64], high[:, 64 * g : 64 * g + 64]], axis=1)
        for t in range(8):
            out_ref[g * 8 + t, AREA:SLOT_ROWS, :] = tile[40 * t : 40 * t + 40].astype(BF16)


def rim_kernel(wet_hbm, diff_hbm, grid_hbm, up_ref, down_ref, wet_ref, diff_ref, rows_ref, sems):
    pairs = [(wet_hbm, wet_ref), (diff_hbm, diff_ref), (grid_hbm.at[0:2], rows_ref.at[0:2]),
             (grid_hbm.at[18:20], rows_ref.at[2:4])]
    copies = [pltpu.make_async_copy(a, b, sems.at[i]) for i, (a, b) in enumerate(pairs)]
    for c in copies:
        c.start()
    for c in copies:
        c.wait()
    row8 = iota((8, 640), 0)
    for n, (ref, first) in enumerate(((up_ref, 0), (down_ref, 18))):
        for i in range(2):
            r = first + i
            wet = wet_ref[r : r + 1, :].astype(F32)
            hi, lo = split_hi_lo(diff_ref[r : r + 1, :] * wet)
            extra = jnp.zeros((8, 640), F32)
            for m, x in enumerate((wet, hi, lo)):
                extra = jnp.where(row8 == m, x, extra)
            ref[i, 0:32, :] = rows_ref[2 * n + i]
            ref[i, 32:40, :] = extra.astype(BF16)


def remap_kernel(list_ref, recv_ref, wgt_ref, wet_ref, diff_ref,
                 rec_ref, tail_ref, planes_ref, up_ref, down_ref):
    me_grp, me_lon = lax.axis_index("grp"), lax.axis_index("lon")
    slot_l = me_grp * 8 + ((me_lon + 7) & 7)
    slot_r = me_grp * 8 + ((me_lon + 1) & 7)
    row8 = iota((8, 1), 0)

    def ids(k, s, centre):
        h = (k >= 3).astype(I32) + (k >= 6).astype(I32) + (k >= 9).astype(I32)
        lon = (centre + k - 3 * h + 7) & 7
        row = (s * 205) >> 10
        return h * 8 + lon, (s - 5 * row) * 20 + row

    lists = [tuple(upright(list_ref[c]) for c in range(3))]
    for slot in (slot_l, slot_r):
        rows = recv_ref[slot, ROW_LIST : ROW_LIST + 8, :].astype(F32).astype(I32)
        lists.append((rows[:, 0:1], rows[:, 1:2], rows[:, 2:3]))
    pairs = [ids(k, s, me_lon + shift) for (k, s, _), shift in zip(lists, (0, 7, 1))]
    slot_id = jnp.concatenate([p[0] for p in pairs], axis=0)
    block_id = jnp.concatenate([p[1] for p in pairs], axis=0)
    in_block = jnp.where(iota((24, 104), 1) == block_id, 1.0, 0.0)
    source = jnp.zeros((24, 128), F32)
    for slot in range(32):
        pick = jnp.where(slot_id == slot, in_block, 0.0).astype(BF16)
        source += mm(pick, recv_ref[slot, 0:AREA, :])
    own = source[0:8].astype(BF16)
    prod = jnp.zeros((8, 128), F32)
    for e in range(8):
        prod = jnp.where(row8 == e, mm(own, wgt_ref[e], NT), prod)
    target = lists[0][2]
    trow = (target * 205) >> 10
    place = jnp.where(iota((8, 256), 1) == (target - 5 * trow) * 32 + trow, 1.0, 0.0)
    placed = mm(place, prod, TN, lax.Precision.HIGHEST)
    received = jnp.concatenate([placed[32 * c : 32 * c + 20] for c in range(5)], axis=1)
    rec_ref[...] = received
    lane = iota((8, 128), 1)
    values, spots = [], []
    for n, (slot, lane0, col) in enumerate(((slot_l, 126, 4), (slot_r, 0, 0))):
        rows = recv_ref[slot, ROW_WGT:ROW_LIST, :].astype(F32)
        src = source[8 + 8 * n : 16 + 8 * n]
        v0 = jnp.sum(rows[0:8] * src, axis=1, keepdims=True)
        v1 = jnp.sum(rows[8:16] * src, axis=1, keepdims=True)
        values.append(jnp.where(lane == lane0, v0, 0.0) + jnp.where(lane == lane0 + 1, v1, 0.0))
        goal = lists[1 + n][2]
        grow = (goal * 205) >> 10
        spots.append(jnp.where((lane == grow) & (goal - 5 * grow == col), 1.0, 0.0))
    rec_tail = mm(jnp.concatenate(spots, axis=0), jnp.concatenate(values, axis=0), TN, lax.Precision.HIGHEST)[0:20]
    edge = jnp.concatenate(
        [recv_ref[slot_l, 0:ROW_WGT, :].astype(F32), recv_ref[slot_r, 0:ROW_WGT, :].astype(F32)], axis=0
    ).astype(BF16)
    r32, l32 = iota((32, 128), 0), iota((32, 128), 1)

    def tail_of(k):
        pick = onehot(
            ((r32 == k) & (l32 == 126)) | ((r32 == 8 + k) & (l32 == 127))
            | ((r32 == 16 + k) & (l32 == 0)) | ((r32 == 24 + k) & (l32 == 1))
        )
        return mm(edge, pick, TN)

    for k in range(5):
        tail_ref[4 * k : 4 * k + 4] = tail_of(k).reshape(4, 32, 128).astype(BF16)
    last = tail_of(5)
    own_wet = wet_ref[...].astype(F32)
    wet = jnp.concatenate([own_wet, last[0:20]], axis=1)
    dif = jnp.concatenate([diff_ref[...] * own_wet, last[32:52] + last[64:84]], axis=1)
    force = wet * jnp.concatenate([received, rec_tail], axis=1)
    planes_ref[0] = wet
    planes_ref[1] = dif
    planes_ref[2] = force
    fhi, flo = split_hi_lo(force)
    row16 = iota((16, 128), 0)
    for ref, first in ((up_ref, 0), (down_ref, 18)):
        for i in range(2):
            r = first + i
            ref[i, 0:32, :] = tail_ref[r]
            extra = jnp.zeros((16, 128), F32)
            lines = [x[r : r + 1, 128 * c : 128 * c + 128] for x in (fhi, flo) for c in range(6)]
            lines += [last[r : r + 1], last[32 + r : 33 + r], last[64 + r : 65 + r]]
            for m, x in enumerate(lines):
                extra = jnp.where(row16 == m, x, extra)
            ref[i, 32:48, :] = extra.astype(BF16)


def step_kernel(tail_ref, planes_ref, above_ref, below_ref, above2_ref, below2_ref, grid_ref,
                out_hbm, q_ref, u_ref, q1_ref, u1_ref, wet_ref, dif_ref, c_ref, res_ref, sems):
    level0 = iota((8, WIDE), 0) == 0

    def load(r, row, end, wet, dif, force):
        wet = jnp.broadcast_to(wet, (8, WIDE))
        wet_ref[r] = wet
        dif_ref[r] = jnp.broadcast_to(dif, (8, WIDE))
        cells = jnp.concatenate([row.astype(F32), end.astype(F32)], axis=1)
        for v in range(4):
            part = cells[8 * v : 8 * v + 8]
            if v == 0:
                part = jnp.where(level0, part + force, part)
            q_ref[r, 8 * v : 8 * v + 8, :] = part
            u_ref[r, 8 * v : 8 * v + 8, :] = part * wet

    for ref, ref2, base in ((above_ref, above2_ref, 0), (below_ref, below2_ref, 22)):
        for i in range(2):
            near = ref[i, 32:40, :].astype(F32)
            far = ref2[i, 32:48, :].astype(F32)
            wet = jnp.concatenate([near[0:1], far[12:13]], axis=1)
            dif = jnp.concatenate([near[1:2] + near[2:3], far[13:14] + far[14:15]], axis=1)
            force = jnp.concatenate([far[c : c + 1] + far[6 + c : 7 + c] for c in range(6)], axis=1)
            load(base + i, ref[i, 0:32, :], ref2[i, 0:32, :], wet, dif, force)
    for r in range(20):
        load(r + 2, grid_ref[r], tail_ref[r], planes_ref[0, r : r + 1, :], planes_ref[1, r : r + 1, :],
             planes_ref[2, r : r + 1, :])

    def sides(x):
        return pltpu.roll(x, 1, axis=1) + pltpu.roll(x, WIDE - 1, axis=1)

    def first(r, carry):
        dif = dif_ref[r]
        wet = wet_ref[r]
        coef = 1.0 - dif * (wet_ref[r - 1] + wet_ref[r + 1] + sides(wet))
        c_ref[r] = coef
        for v in range(4):
            lev = pl.ds(8 * v, 8)
            total = sides(u_ref[r, lev, :]) + u_ref[r - 1, lev, :] + u_ref[r + 1, lev, :]
            q = q_ref[r, lev, :] * coef + dif * total
            q1_ref[r, lev, :] = q
            u1_ref[r, lev, :] = q * wet
        return carry

    lax.fori_loop(1, 23, first, 0)

    def copy(r):
        return pltpu.make_async_copy(res_ref.at[r], out_hbm.at[r], sems.at[r])

    def second(r, carry):
        coef = c_ref[r]
        dif = dif_ref[r]
        for v in range(4):
            lev = pl.ds(8 * v, 8)
            total = sides(u1_ref[r, lev, :]) + u1_ref[r - 1, lev, :] + u1_ref[r + 1, lev, :]
            q = q1_ref[r, lev, :] * coef + dif * total
            res_ref[r - 2, lev, :] = q[:, 0:640]
        copy(r - 2).start()
        return carry

    lax.fori_loop(2, 22, second, 0)

    def finish(r, carry):
        copy(r).wait()
        return carry

    lax.fori_loop(0, 20, finish, 0)


def turn_kernel(recv_ref, out_ref):
    norm = np.float32(1.0 / math.sqrt(5120.0))
    sums = []
    for g in range(3):
        acc = recv_ref[g * 8, AREA:SLOT_ROWS, :].astype(F32)
        for t in range(1, 8):
            acc += recv_ref[g * 8 + t, AREA:SLOT_ROWS, :].astype(F32)
        sums.append(acc)
    stack = (jnp.concatenate(sums + [jnp.zeros((8, 128), F32)], axis=0) * norm).astype(BF16)
    out = jnp.zeros((256, 128), F32)
    for j2 in range(2):
        lane = iota((128, 128), 0)
        g = (lane >= 20).astype(I32) + (lane >= 40).astype(I32)
        pick = onehot((iota((128, 128), 1) == lane + 20 * g + 20 * j2) & (lane < 60))
        lined = mm(pick, stack).astype(BF16)
        rho, lam = iota((256, 128), 0), iota((256, 128), 1)
        want = ((rho >> 2) & 1) * 64 + (rho & 1) * 32 + (rho >> 3)
        place = onehot((((rho >> 1) & 1) == j2) & (lam == want))
        out += mm(place, lined, NT)
    out_ref[...] = out.astype(BF16)


def legendre_kernel(waves_ref, table_hbm, out_ref, table_ref, sems):
    copies = [
        pltpu.make_async_copy(table_hbm.at[pl.ds(128 * i, 128), :], table_ref.at[pl.ds(128 * i, 128), :], sems.at[i])
        for i in range(15)
    ]
    for c in copies:
        c.start()
    lane = iota((8, 128), 1)
    waves = [waves_ref[l].astype(F32) for l in range(32)]
    tiles = []
    for tau in range(15):
        tile = jnp.zeros((8, 128), F32)
        for g in range(3):
            for l in range(32):
                start = g * 640 + l * 20 - 128 * tau
                if start <= -20 or start >= 128:
                    continue
                shift = (start - 20 * g) % 128
                moved = pltpu.roll(waves[l], shift, axis=1) if shift else waves[l]
                tile = jnp.where((lane >= start) & (lane < start + 20), moved, tile)
        tiles.append(tile)
    out = jnp.zeros((8, 1280), F32)
    left = jnp.concatenate(tiles, axis=1).astype(BF16)
    for i in range(0, 15, 2):
        for c in copies[i : i + 2]:
            c.wait()
        k = min(256, 1920 - 128 * i)
        out += mm(left[:, 128 * i : 128 * i + k], table_ref[128 * i : 128 * i + k, :])
    for j in range(4):
        out_ref[j] = out[2 * j : 2 * j + 2]


VMEM = pl.BlockSpec(memory_space=pltpu.VMEM)
SMEM = pl.BlockSpec(memory_space=pltpu.SMEM)
HBM = pl.BlockSpec(memory_space=pltpu.HBM)


def call(kernel, name, smem, vmem, hbm, outs, scratch=(), out_space=VMEM, limit=None):
    flat = [jax.ShapeDtypeStruct(s, d) for s, d in outs]
    return pl.pallas_call(
        kernel,
        name=name,
        out_shape=flat if len(flat) > 1 else flat[0],
        in_specs=[SMEM] * len(smem) + [VMEM] * len(vmem) + [HBM] * len(hbm),
        out_specs=[out_space] * len(flat) if len(flat) > 1 else out_space,
        scratch_shapes=list(scratch),
        compiler_params=pltpu.CompilerParams(vmem_limit_bytes=limit and limit * 1024 * 1024),
    )(*smem, *vmem, *hbm)


def trig_tables():
    phase = np.arange(128)[:, None] * np.arange(640)[None, :] % 5120
    angle = 2.0 * np.pi / 5120.0 * phase
    return np.cos(angle).astype(np.float32), np.sin(angle).astype(np.float32)


def shards(grid_state, legendre, sent_field, wet_mask, diffusivity, remap_blocks, remap_weights):
    rows = grid_state.transpose(1, 0, 2)
    listing = remap_blocks.transpose(0, 3, 1, 2).reshape(3, 1, 8)
    weights = remap_weights[0, 0]
    bands = lax.axis_size(("grp", "lat"))
    to_before = [((i + 1) % bands, i) for i in range(bands)]
    to_after = [(i, (i + 1) % bands) for i in range(bands)]
    cos0, sin0 = trig_tables()
    packed = call(
        pack_kernel, "pack", (), (),
        (jnp.asarray(cos0), jnp.asarray(sin0), listing, rows, sent_field, wet_mask, diffusivity, weights),
        [((32, SLOT_ROWS, 128), BF16)],
        scratch=[pltpu.VMEM((128, 640), F32), pltpu.VMEM((128, 640), F32), pltpu.VMEM((3, 1, 8), I32), pltpu.VMEM((20, 32, 640), BF16),
                 pltpu.VMEM((20, 640), F32), pltpu.VMEM((20, 640), I32), pltpu.VMEM((20, 640), F32),
                 pltpu.VMEM((2, 8, 16, 128), BF16), pltpu.SemaphoreType.DMA((9,))],
    )
    plane = lax.all_to_all(packed, ("grp", "lon"), 0, 0, tiled=True)
    up, down = call(
        rim_kernel, "rim", (), (), (wet_mask, diffusivity, rows),
        [((2, 40, 640), BF16), ((2, 40, 640), BF16)],
        scratch=[pltpu.VMEM((20, 640), I32), pltpu.VMEM((20, 640), F32), pltpu.VMEM((4, 32, 640), BF16),
                 pltpu.SemaphoreType.DMA((4,))],
    )
    below = lax.ppermute(up, ("grp", "lat"), to_before)
    above = lax.ppermute(down, ("grp", "lat"), to_after)
    plane, above, below = lax.optimization_barrier((plane, above, below))
    turned = call(turn_kernel, "turn", (), (plane,), (), [((256, 128), BF16)], limit=16)
    waves = lax.all_to_all(turned.reshape(32, 8, 128), "lat", 0, 0, tiled=True)
    received, tail, planes, up2, down2 = call(
        remap_kernel, "remap", (), (listing, plane, weights, wet_mask, diffusivity), (),
        [((20, 640), F32), ((20, 32, 128), BF16), ((3, 20, WIDE), F32), ((2, 48, 128), BF16), ((2, 48, 128), BF16)],
        limit=16,
    )
    below2 = lax.ppermute(up2, ("grp", "lat"), to_before)
    above2 = lax.ppermute(down2, ("grp", "lat"), to_after)
    stepped = call(
        step_kernel, "step", (), (tail, planes, above, below, above2, below2, rows), (),
        [((20, 32, 640), F32)],
        scratch=[pltpu.VMEM((24, 32, WIDE), F32)] * 4 + [pltpu.VMEM((24, 8, WIDE), F32)] * 3
        + [pltpu.VMEM((20, 32, 640), F32), pltpu.SemaphoreType.DMA((20,))],
        out_space=HBM, limit=32,
    )
    table, stepped = lax.optimization_barrier((legendre[0], stepped))
    spectral = call(
        legendre_kernel, "legendre", (), (waves,), (table,), [((4, 2, 1280), F32)],
        scratch=[pltpu.VMEM((1920, 1280), BF16), pltpu.SemaphoreType.DMA((15,))], limit=60,
    )
    return spectral.reshape(1, 4, 2, 1280), received, stepped.transpose(1, 0, 2)


def solution(mesh):
    in_specs = (
        P(None, ("grp", "lat"), "lon"),
        P(("grp", "lat"), None, None),
        P(("grp", "lat"), "lon"),
        P(("grp", "lat"), "lon"),
        P(("grp", "lat"), "lon"),
        P(("grp", "lat"), "lon", None, None),
        P(("grp", "lat"), "lon", None, None, None),
    )
    out_specs = (
        P(("grp", "lat"), "lon", None, None),
        P(("grp", "lat"), "lon"),
        P(None, ("grp", "lat"), "lon"),
    )
    return jax.shard_map(shards, mesh=mesh, in_specs=in_specs, out_specs=out_specs, check_vma=False)
```

```python
import functools
import math

import jax
import jax.numpy as jnp
import numpy as np
from jax import lax
from jax.experimental import pallas as pl
from jax.experimental.pallas import tpu as pltpu
from jax.sharding import PartitionSpec as P

F32 = jnp.float32
BF16 = jnp.bfloat16
I32 = jnp.int32
NT = (((1,), (1,)), ((), ()))
TN = (((0,), (0,)), ((), ()))

WIDE = 768
ROW_WGT = 16
ROW_LIST = 32
AREA = 104
FIRST_LAT = 16
SLOT_ROWS = 144


def iota(shape, dim):
    return lax.broadcasted_iota(I32, shape, dim)


def onehot(cond):
    return jnp.where(cond, 1.0, 0.0).astype(BF16)


def mm(a, b, dims=(((1,), (0,)), ((), ())), precision=None):
    return lax.dot_general(a, b, dims, preferred_element_type=F32, precision=precision)


def upright(x):
    return jnp.sum(jnp.where(iota((8, 8), 0) == iota((8, 8), 1), x, 0), axis=1, keepdims=True)


def split_hi_lo(x):
    hi = x.astype(BF16).astype(F32)
    return hi, x - hi


def pack_kernel(cos_hbm, sin_hbm, list_hbm, grid_hbm, sent_hbm, wet_hbm, diff_hbm, wgt_hbm,
                out_ref, cos_ref, sin_ref, list_ref, grid_ref, sent_ref, wet_ref, diff_ref, wgt_ref, sems):
    pairs = [(list_hbm, list_ref), (sent_hbm, sent_ref), (wet_hbm, wet_ref), (diff_hbm, diff_ref)]
    pairs += [(wgt_hbm.at[:, pl.ds(112 * side, 16), :], wgt_ref.at[side]) for side in range(2)]
    pairs += [(cos_hbm, cos_ref), (sin_hbm, sin_ref), (grid_hbm, grid_ref)]
    copies = [pltpu.make_async_copy(a, b, sems.at[i]) for i, (a, b) in enumerate(pairs)]
    for c in copies:
        c.start()
    me_lon = lax.axis_index("lon")
    turn = (iota((128, 1), 0) * me_lon) & 7
    half = math.sqrt(0.5)

    def eighth(k):
        values = (1.0, half, 0.0, -half, -1.0, -half, 0.0, half)
        out = jnp.zeros((128, 1), F32)
        for i, v in enumerate(values):
            out = jnp.where(((turn + k) & 7) == i, v, out)
        return out

    cos_t, sin_t = eighth(0), eighth(6)
    rho = iota((640, 1), 0)
    jh = (rho >= 320).astype(I32)
    rem = rho - 320 * jh
    tt = (rem * 205) >> 13
    rem = rem - 40 * tt
    j2 = (rem >= 20).astype(I32)
    source = (rem - 20 * j2) * 32 + 4 * tt + 2 * jh + j2
    order = onehot(iota((640, 640), 1) == source)
    row8, lane8 = iota((8, 128), 0), iota((8, 128), 1)
    for c in copies[:6]:
        c.wait()
    listing = jnp.zeros((8, 128), F32)
    for c in range(3):
        listing = jnp.where(lane8 == c, upright(list_ref[c]).astype(F32), listing)
    sent = sent_ref[...]
    spread = jnp.zeros((104, 128), F32)
    for c in range(5):
        pick = onehot((iota((104, 32), 0) == iota((104, 32), 1) + 20 * c) & (iota((104, 32), 1) < 20))
        block = jnp.concatenate([sent[:, 128 * c : 128 * c + 128], jnp.zeros((12, 128), F32)], axis=0)
        spread += mm(pick, block.astype(BF16))
    wet = wet_ref[...].astype(F32)
    dif = diff_ref[...] * wet
    pad = jnp.zeros((12, 128), F32)
    wgt, planes = [], []
    for side in range(2):
        base = 512 * side
        hi, lo = split_hi_lo(dif[:, base : base + 128])
        planes.append(jnp.concatenate(
            [wet[:, base : base + 128], pad, hi, pad, lo, pad, jnp.zeros((32, 128), F32)], axis=0
        ).astype(BF16))
        for i in range(2):
            rows = jnp.zeros((8, 128), F32)
            for e in range(8):
                rows = jnp.where(row8 == e, wgt_ref[side, e].astype(F32)[14 * side + i : 14 * side + i + 1], rows)
            wgt.append(rows)
    for c in copies[6:8]:
        c.wait()
    cos0, sin0 = cos_ref[...], sin_ref[...]
    cos_m = cos_t * cos0 - sin_t * sin0
    sin_m = -(sin_t * cos0 + cos_t * sin0)
    parts = []
    for g in range(4):
        parts += [cos_m[32 * g : 32 * g + 32], sin_m[32 * g : 32 * g + 32]]
    basis = jnp.concatenate(parts, axis=0).astype(BF16)
    copies[8].wait()
    sums = mm(grid_ref[...].reshape(640, 640), basis, NT).astype(BF16)
    blocks = []
    for side in range(2):
        base, lane0 = 512 * side, 126 * side
        edge = jnp.zeros((16, 128), F32)
        for k in range(6):
            src = grid_ref[4 * k : 4 * k + 4, :, base : base + 128].reshape(128, 128) if k < 5 else planes[side]
            r16, l16 = iota((16, 128), 0), iota((16, 128), 1)
            pick = onehot(((r16 == k) & (l16 == lane0)) | ((r16 == 8 + k) & (l16 == lane0 + 1)))
            edge += mm(pick, src, NT)
        pieces = [edge, wgt[2 * side], wgt[2 * side + 1], listing, jnp.zeros((AREA - 40, 128), F32)]
        blocks.append(jnp.concatenate(pieces, axis=0))
    for g in range(4):
        same = lax.axis_index("grp") == g
        left = jnp.where(same, blocks[0], spread)
        right = jnp.where(same, blocks[1], spread)
        for t in range(8):
            to_left = ((me_lon + 7) & 7) == t
            out_ref[g * 8 + t, 0:AREA, :] = jnp.where(to_left, left, right).astype(BF16)
    moved = mm(order, sums)
    low, high = moved[:320], moved[320:]
    for g in range(4):
        tile = jnp.concatenate([low[:, 64 * g : 64 * g + 64], high[:, 64 * g : 64 * g + 64]], axis=1)
        for t in range(8):
            out_ref[g * 8 + t, AREA:SLOT_ROWS, :] = tile[40 * t : 40 * t + 40].astype(BF16)


def rim_kernel(wet_hbm, diff_hbm, grid_hbm, up_ref, down_ref, wet_ref, diff_ref, rows_ref, sems):
    pairs = [(wet_hbm, wet_ref), (diff_hbm, diff_ref), (grid_hbm.at[0:2], rows_ref.at[0:2]),
             (grid_hbm.at[18:20], rows_ref.at[2:4])]
    copies = [pltpu.make_async_copy(a, b, sems.at[i]) for i, (a, b) in enumerate(pairs)]
    for c in copies:
        c.start()
    for c in copies:
        c.wait()
    row8 = iota((8, 640), 0)
    for n, (ref, first) in enumerate(((up_ref, 0), (down_ref, 18))):
        for i in range(2):
            r = first + i
            wet = wet_ref[r : r + 1, :].astype(F32)
            hi, lo = split_hi_lo(diff_ref[r : r + 1, :] * wet)
            extra = jnp.zeros((8, 640), F32)
            for m, x in enumerate((wet, hi, lo)):
                extra = jnp.where(row8 == m, x, extra)
            ref[i, 0:32, :] = rows_ref[2 * n + i]
            ref[i, 32:40, :] = extra.astype(BF16)


def remap_kernel(list_ref, recv_ref, wgt_ref, wet_ref, diff_ref,
                 rec_ref, tail_ref, planes_ref, up_ref, down_ref):
    me_grp, me_lon = lax.axis_index("grp"), lax.axis_index("lon")
    slot_l = me_grp * 8 + ((me_lon + 7) & 7)
    slot_r = me_grp * 8 + ((me_lon + 1) & 7)
    row8 = iota((8, 1), 0)

    def ids(k, s, centre):
        h = (k >= 3).astype(I32) + (k >= 6).astype(I32) + (k >= 9).astype(I32)
        lon = (centre + k - 3 * h + 7) & 7
        row = (s * 205) >> 10
        return h * 8 + lon, (s - 5 * row) * 20 + row

    lists = [tuple(upright(list_ref[c]) for c in range(3))]
    for slot in (slot_l, slot_r):
        rows = recv_ref[slot, ROW_LIST : ROW_LIST + 8, :].astype(F32).astype(I32)
        lists.append((rows[:, 0:1], rows[:, 1:2], rows[:, 2:3]))
    pairs = [ids(k, s, me_lon + shift) for (k, s, _), shift in zip(lists, (0, 7, 1))]
    slot_id = jnp.concatenate([p[0] for p in pairs], axis=0)
    block_id = jnp.concatenate([p[1] for p in pairs], axis=0)
    in_block = jnp.where(iota((24, 104), 1) == block_id, 1.0, 0.0)
    source = jnp.zeros((24, 128), F32)
    for slot in range(32):
        pick = jnp.where(slot_id == slot, in_block, 0.0).astype(BF16)
        source += mm(pick, recv_ref[slot, 0:AREA, :])
    own = source[0:8].astype(BF16)
    prod = jnp.zeros((8, 128), F32)
    for e in range(8):
        prod = jnp.where(row8 == e, mm(own, wgt_ref[e], NT), prod)
    target = lists[0][2]
    trow = (target * 205) >> 10
    place = jnp.where(iota((8, 256), 1) == (target - 5 * trow) * 32 + trow, 1.0, 0.0)
    placed = mm(place, prod, TN, lax.Precision.HIGHEST)
    received = jnp.concatenate([placed[32 * c : 32 * c + 20] for c in range(5)], axis=1)
    rec_ref[...] = received
    lane = iota((8, 128), 1)
    values, spots = [], []
    for n, (slot, lane0, col) in enumerate(((slot_l, 126, 4), (slot_r, 0, 0))):
        rows = recv_ref[slot, ROW_WGT:ROW_LIST, :].astype(F32)
        src = source[8 + 8 * n : 16 + 8 * n]
        v0 = jnp.sum(rows[0:8] * src, axis=1, keepdims=True)
        v1 = jnp.sum(rows[8:16] * src, axis=1, keepdims=True)
        values.append(jnp.where(lane == lane0, v0, 0.0) + jnp.where(lane == lane0 + 1, v1, 0.0))
        goal = lists[1 + n][2]
        grow = (goal * 205) >> 10
        spots.append(jnp.where((lane == grow) & (goal - 5 * grow == col), 1.0, 0.0))
    rec_tail = mm(jnp.concatenate(spots, axis=0), jnp.concatenate(values, axis=0), TN, lax.Precision.HIGHEST)[0:20]
    edge = jnp.concatenate(
        [recv_ref[slot_l, 0:ROW_WGT, :].astype(F32), recv_ref[slot_r, 0:ROW_WGT, :].astype(F32)], axis=0
    ).astype(BF16)
    r32, l32 = iota((32, 128), 0), iota((32, 128), 1)

    def tail_of(k):
        pick = onehot(
            ((r32 == k) & (l32 == 126)) | ((r32 == 8 + k) & (l32 == 127))
            | ((r32 == 16 + k) & (l32 == 0)) | ((r32 == 24 + k) & (l32 == 1))
        )
        return mm(edge, pick, TN)

    for k in range(5):
        tail_ref[4 * k : 4 * k + 4] = tail_of(k).reshape(4, 32, 128).astype(BF16)
    last = tail_of(5)
    own_wet = wet_ref[...].astype(F32)
    wet = jnp.concatenate([own_wet, last[0:20]], axis=1)
    dif = jnp.concatenate([diff_ref[...] * own_wet, last[32:52] + last[64:84]], axis=1)
    force = wet * jnp.concatenate([received, rec_tail], axis=1)
    planes_ref[0] = wet
    planes_ref[1] = dif
    planes_ref[2] = force
    fhi, flo = split_hi_lo(force)
    row16 = iota((16, 128), 0)
    for ref, first in ((up_ref, 0), (down_ref, 18)):
        for i in range(2):
            r = first + i
            ref[i, 0:32, :] = tail_ref[r]
            extra = jnp.zeros((16, 128), F32)
            lines = [x[r : r + 1, 128 * c : 128 * c + 128] for x in (fhi, flo) for c in range(6)]
            lines += [last[r : r + 1], last[32 + r : 33 + r], last[64 + r : 65 + r]]
            for m, x in enumerate(lines):
                extra = jnp.where(row16 == m, x, extra)
            ref[i, 32:48, :] = extra.astype(BF16)


def step_kernel(tail_ref, planes_ref, above_ref, below_ref, above2_ref, below2_ref, grid_ref,
                out_hbm, q_ref, u_ref, q1_ref, u1_ref, wet_ref, dif_ref, c_ref, res_ref, sems):
    level0 = iota((8, WIDE), 0) == 0

    def load(r, row, end, wet, dif, force):
        wet = jnp.broadcast_to(wet, (8, WIDE))
        wet_ref[r] = wet
        dif_ref[r] = jnp.broadcast_to(dif, (8, WIDE))
        cells = jnp.concatenate([row.astype(F32), end.astype(F32)], axis=1)
        for v in range(4):
            part = cells[8 * v : 8 * v + 8]
            if v == 0:
                part = jnp.where(level0, part + force, part)
            q_ref[r, 8 * v : 8 * v + 8, :] = part
            u_ref[r, 8 * v : 8 * v + 8, :] = part * wet

    for ref, ref2, base in ((above_ref, above2_ref, 0), (below_ref, below2_ref, 22)):
        for i in range(2):
            near = ref[i, 32:40, :].astype(F32)
            far = ref2[i, 32:48, :].astype(F32)
            wet = jnp.concatenate([near[0:1], far[12:13]], axis=1)
            dif = jnp.concatenate([near[1:2] + near[2:3], far[13:14] + far[14:15]], axis=1)
            force = jnp.concatenate([far[c : c + 1] + far[6 + c : 7 + c] for c in range(6)], axis=1)
            load(base + i, ref[i, 0:32, :], ref2[i, 0:32, :], wet, dif, force)
    for r in range(20):
        load(r + 2, grid_ref[r], tail_ref[r], planes_ref[0, r : r + 1, :], planes_ref[1, r : r + 1, :],
             planes_ref[2, r : r + 1, :])

    def sides(x):
        return pltpu.roll(x, 1, axis=1) + pltpu.roll(x, WIDE - 1, axis=1)

    def first(r, carry):
        dif = dif_ref[r]
        wet = wet_ref[r]
        coef = 1.0 - dif * (wet_ref[r - 1] + wet_ref[r + 1] + sides(wet))
        c_ref[r] = coef
        for v in range(4):
            lev = pl.ds(8 * v, 8)
            total = sides(u_ref[r, lev, :]) + u_ref[r - 1, lev, :] + u_ref[r + 1, lev, :]
            q = q_ref[r, lev, :] * coef + dif * total
            q1_ref[r, lev, :] = q
            u1_ref[r, lev, :] = q * wet
        return carry

    lax.fori_loop(1, 23, first, 0)

    def copy(r):
        return pltpu.make_async_copy(res_ref.at[r], out_hbm.at[r], sems.at[r])

    def second(r, carry):
        coef = c_ref[r]
        dif = dif_ref[r]
        for v in range(4):
            lev = pl.ds(8 * v, 8)
            total = sides(u1_ref[r, lev, :]) + u1_ref[r - 1, lev, :] + u1_ref[r + 1, lev, :]
            q = q1_ref[r, lev, :] * coef + dif * total
            res_ref[r - 2, lev, :] = q[:, 0:640]
        copy(r - 2).start()
        return carry

    lax.fori_loop(2, 22, second, 0)

    def finish(r, carry):
        copy(r).wait()
        return carry

    lax.fori_loop(0, 20, finish, 0)


def turn_kernel(recv_ref, out_ref):
    norm = np.float32(1.0 / math.sqrt(5120.0))
    sums = []
    for g in range(3):
        acc = recv_ref[g * 8, AREA:SLOT_ROWS, :].astype(F32)
        for t in range(1, 8):
            acc += recv_ref[g * 8 + t, AREA:SLOT_ROWS, :].astype(F32)
        sums.append(acc)
    stack = (jnp.concatenate(sums + [jnp.zeros((8, 128), F32)], axis=0) * norm).astype(BF16)
    out = jnp.zeros((256, 128), F32)
    for j2 in range(2):
        lane = iota((128, 128), 0)
        g = (lane >= 20).astype(I32) + (lane >= 40).astype(I32)
        pick = onehot((iota((128, 128), 1) == lane + 20 * g + 20 * j2) & (lane < 60))
        lined = mm(pick, stack).astype(BF16)
        rho, lam = iota((256, 128), 0), iota((256, 128), 1)
        want = ((rho >> 2) & 1) * 64 + (rho & 1) * 32 + (((rho >> 3) + FIRST_LAT) & 31)
        place = onehot((((rho >> 1) & 1) == j2) & (lam == want))
        out += mm(place, lined, NT)
    out_ref[...] = out.astype(BF16)


def legendre_kernel(waves_hbm, table_hbm, out_ref, waves_ref, table_ref, sems):
    copies = [
        pltpu.make_async_copy(table_hbm.at[pl.ds(128 * i, 128), :], table_ref.at[pl.ds(128 * i, 128), :], sems.at[i])
        for i in range(15)
    ]
    first = pltpu.make_async_copy(waves_hbm, waves_ref, sems.at[15])
    first.start()
    for c in copies:
        c.start()
    first.wait()
    lane = iota((8, 128), 1)
    waves = [waves_ref[(l - FIRST_LAT) % 32].astype(F32) for l in range(32)]
    tiles = []
    for tau in range(15):
        tile = jnp.zeros((8, 128), F32)
        for g in range(3):
            for l in range(32):
                start = g * 640 + l * 20 - 128 * tau
                if start <= -20 or start >= 128:
                    continue
                shift = (start - 20 * g) % 128
                moved = pltpu.roll(waves[l], shift, axis=1) if shift else waves[l]
                tile = jnp.where((lane >= start) & (lane < start + 20), moved, tile)
        tiles.append(tile)
    out = jnp.zeros((8, 1280), F32)
    for i in range(15):
        copies[i].wait()
        out += mm(tiles[i].astype(BF16), table_ref[128 * i : 128 * i + 128, :])
    for j in range(4):
        out_ref[j] = out[2 * j : 2 * j + 2]


VMEM = pl.BlockSpec(memory_space=pltpu.VMEM)
SMEM = pl.BlockSpec(memory_space=pltpu.SMEM)
HBM = pl.BlockSpec(memory_space=pltpu.HBM)


def call(kernel, name, smem, vmem, hbm, outs, scratch=(), out_space=VMEM, limit=None):
    flat = [jax.ShapeDtypeStruct(s, d) for s, d in outs]
    return pl.pallas_call(
        kernel,
        name=name,
        out_shape=flat if len(flat) > 1 else flat[0],
        in_specs=[SMEM] * len(smem) + [VMEM] * len(vmem) + [HBM] * len(hbm),
        out_specs=[out_space] * len(flat) if len(flat) > 1 else out_space,
        scratch_shapes=list(scratch),
        compiler_params=pltpu.CompilerParams(vmem_limit_bytes=limit and limit * 1024 * 1024),
    )(*smem, *vmem, *hbm)


def trig_tables():
    phase = np.arange(128)[:, None] * np.arange(640)[None, :] % 5120
    angle = 2.0 * np.pi / 5120.0 * phase
    return np.cos(angle).astype(np.float32), np.sin(angle).astype(np.float32)


def shards(grid_state, legendre, sent_field, wet_mask, diffusivity, remap_blocks, remap_weights):
    rows = grid_state.transpose(1, 0, 2)
    listing = remap_blocks.transpose(0, 3, 1, 2).reshape(3, 1, 8)
    weights = remap_weights[0, 0]
    bands = lax.axis_size(("grp", "lat"))
    to_before = [((i + 1) % bands, i) for i in range(bands)]
    to_after = [(i, (i + 1) % bands) for i in range(bands)]
    cos0, sin0 = trig_tables()
    packed = call(
        pack_kernel, "pack", (), (),
        (jnp.asarray(cos0), jnp.asarray(sin0), listing, rows, sent_field, wet_mask, diffusivity, weights),
        [((32, SLOT_ROWS, 128), BF16)],
        scratch=[pltpu.VMEM((128, 640), F32), pltpu.VMEM((128, 640), F32), pltpu.VMEM((3, 1, 8), I32), pltpu.VMEM((20, 32, 640), BF16),
                 pltpu.VMEM((20, 640), F32), pltpu.VMEM((20, 640), I32), pltpu.VMEM((20, 640), F32),
                 pltpu.VMEM((2, 8, 16, 128), BF16), pltpu.SemaphoreType.DMA((9,))],
    )
    plane = lax.all_to_all(packed, ("grp", "lon"), 0, 0, tiled=True)
    up, down = call(
        rim_kernel, "rim", (), (), (wet_mask, diffusivity, rows),
        [((2, 40, 640), BF16), ((2, 40, 640), BF16)],
        scratch=[pltpu.VMEM((20, 640), I32), pltpu.VMEM((20, 640), F32), pltpu.VMEM((4, 32, 640), BF16),
                 pltpu.SemaphoreType.DMA((4,))],
    )
    below = lax.ppermute(up, ("grp", "lat"), to_before)
    above = lax.ppermute(down, ("grp", "lat"), to_after)
    plane, above, below = lax.optimization_barrier((plane, above, below))
    turned = call(turn_kernel, "turn", (), (plane,), (), [((256, 128), BF16)], limit=16)
    waves = lax.all_to_all(
        turned.reshape(32, 8, 128), "lat", 0, 0, tiled=True, axis_index_groups=[[(i + FIRST_LAT) % 32 for i in range(32)]]
    )
    received, tail, planes, up2, down2 = call(
        remap_kernel, "remap", (), (listing, plane, weights, wet_mask, diffusivity), (),
        [((20, 640), F32), ((20, 32, 128), BF16), ((3, 20, WIDE), F32), ((2, 48, 128), BF16), ((2, 48, 128), BF16)],
        limit=16,
    )
    below2 = lax.ppermute(up2, ("grp", "lat"), to_before)
    above2 = lax.ppermute(down2, ("grp", "lat"), to_after)
    stepped = call(
        step_kernel, "step", (), (tail, planes, above, below, above2, below2, rows), (),
        [((20, 32, 640), F32)],
        scratch=[pltpu.VMEM((24, 32, WIDE), F32)] * 4 + [pltpu.VMEM((24, 8, WIDE), F32)] * 3
        + [pltpu.VMEM((20, 32, 640), F32), pltpu.SemaphoreType.DMA((20,))],
        out_space=HBM, limit=32,
    )
    table, stepped = lax.optimization_barrier((legendre[0], stepped))
    spectral = call(
        legendre_kernel, "legendre", (), (), (waves, table), [((4, 2, 1280), F32)],
        scratch=[pltpu.VMEM((32, 8, 128), BF16), pltpu.VMEM((1920, 1280), BF16), pltpu.SemaphoreType.DMA((16,))],
    )
    return spectral.reshape(1, 4, 2, 1280), received, stepped.transpose(1, 0, 2)


def solution(mesh):
    in_specs = (
        P(None, ("grp", "lat"), "lon"),
        P(("grp", "lat"), None, None),
        P(("grp", "lat"), "lon"),
        P(("grp", "lat"), "lon"),
        P(("grp", "lat"), "lon"),
        P(("grp", "lat"), "lon", None, None),
        P(("grp", "lat"), "lon", None, None, None),
    )
    out_specs = (
        P(("grp", "lat"), "lon", None, None),
        P(("grp", "lat"), "lon"),
        P(None, ("grp", "lat"), "lon"),
    )
    return jax.shard_map(shards, mesh=mesh, in_specs=in_specs, out_specs=out_specs, check_vma=False)
```

```python
import functools
import math

import jax
import jax.numpy as jnp
import numpy as np
from jax import lax
from jax.experimental import pallas as pl
from jax.experimental.pallas import tpu as pltpu
from jax.sharding import PartitionSpec as P

F32 = jnp.float32
BF16 = jnp.bfloat16
I32 = jnp.int32
NT = (((1,), (1,)), ((), ()))
TN = (((0,), (0,)), ((), ()))

WIDE = 768
ROW_WGT = 16
ROW_LIST = 32
AREA = 104
FIRST_LAT = 23
SLOT_ROWS = 144


def iota(shape, dim):
    return lax.broadcasted_iota(I32, shape, dim)


def onehot(cond):
    return jnp.where(cond, 1.0, 0.0).astype(BF16)


def mm(a, b, dims=(((1,), (0,)), ((), ())), precision=None):
    return lax.dot_general(a, b, dims, preferred_element_type=F32, precision=precision)


def upright(x):
    return jnp.sum(jnp.where(iota((8, 8), 0) == iota((8, 8), 1), x, 0), axis=1, keepdims=True)


def split_hi_lo(x):
    hi = x.astype(BF16).astype(F32)
    return hi, x - hi


def pack_kernel(cos_hbm, sin_hbm, list_hbm, grid_hbm, sent_hbm, wet_hbm, diff_hbm, wgt_hbm,
                out_hbm, out_ref, cos_ref, sin_ref, list_ref, grid_ref, sent_ref, wet_ref, diff_ref, wgt_ref, sems, out_sems):
    pairs = [(list_hbm, list_ref), (sent_hbm, sent_ref), (wet_hbm, wet_ref), (diff_hbm, diff_ref)]
    pairs += [(wgt_hbm.at[:, pl.ds(112 * side, 16), :], wgt_ref.at[side]) for side in range(2)]
    pairs += [(cos_hbm, cos_ref), (sin_hbm, sin_ref), (grid_hbm, grid_ref)]
    copies = [pltpu.make_async_copy(a, b, sems.at[i]) for i, (a, b) in enumerate(pairs)]
    for c in copies:
        c.start()
    me_lon = lax.axis_index("lon")
    turn = (iota((128, 1), 0) * me_lon) & 7
    half = math.sqrt(0.5)

    def eighth(k):
        values = (1.0, half, 0.0, -half, -1.0, -half, 0.0, half)
        out = jnp.zeros((128, 1), F32)
        for i, v in enumerate(values):
            out = jnp.where(((turn + k) & 7) == i, v, out)
        return out

    cos_t, sin_t = eighth(0), eighth(6)
    rho = iota((640, 1), 0)
    jh = (rho >= 320).astype(I32)
    rem = rho - 320 * jh
    tt = (rem * 205) >> 13
    rem = rem - 40 * tt
    j2 = (rem >= 20).astype(I32)
    source = (rem - 20 * j2) * 32 + 4 * tt + 2 * jh + j2
    order = onehot(iota((640, 640), 1) == source)
    row8, lane8 = iota((8, 128), 0), iota((8, 128), 1)
    for c in copies[:6]:
        c.wait()
    listing = jnp.zeros((8, 128), F32)
    for c in range(3):
        listing = jnp.where(lane8 == c, upright(list_ref[c]).astype(F32), listing)
    sent = sent_ref[...]
    spread = jnp.zeros((104, 128), F32)
    for c in range(5):
        pick = onehot((iota((104, 32), 0) == iota((104, 32), 1) + 20 * c) & (iota((104, 32), 1) < 20))
        block = jnp.concatenate([sent[:, 128 * c : 128 * c + 128], jnp.zeros((12, 128), F32)], axis=0)
        spread += mm(pick, block.astype(BF16))
    wet = wet_ref[...].astype(F32)
    dif = diff_ref[...] * wet
    pad = jnp.zeros((12, 128), F32)
    wgt, planes = [], []
    for side in range(2):
        base = 512 * side
        hi, lo = split_hi_lo(dif[:, base : base + 128])
        planes.append(jnp.concatenate(
            [wet[:, base : base + 128], pad, hi, pad, lo, pad, jnp.zeros((32, 128), F32)], axis=0
        ).astype(BF16))
        for i in range(2):
            rows = jnp.zeros((8, 128), F32)
            for e in range(8):
                rows = jnp.where(row8 == e, wgt_ref[side, e].astype(F32)[14 * side + i : 14 * side + i + 1], rows)
            wgt.append(rows)
    for c in copies[6:8]:
        c.wait()
    cos0, sin0 = cos_ref[...], sin_ref[...]
    cos_m = cos_t * cos0 - sin_t * sin0
    sin_m = -(sin_t * cos0 + cos_t * sin0)
    parts = []
    for g in range(4):
        parts += [cos_m[32 * g : 32 * g + 32], sin_m[32 * g : 32 * g + 32]]
    basis = jnp.concatenate(parts, axis=0).astype(BF16)
    copies[8].wait()
    sums = mm(grid_ref[...].reshape(640, 640), basis, NT).astype(BF16)
    blocks = []
    for side in range(2):
        base, lane0 = 512 * side, 126 * side
        edge = jnp.zeros((16, 128), F32)
        for k in range(6):
            src = grid_ref[4 * k : 4 * k + 4, :, base : base + 128].reshape(128, 128) if k < 5 else planes[side]
            r16, l16 = iota((16, 128), 0), iota((16, 128), 1)
            pick = onehot(((r16 == k) & (l16 == lane0)) | ((r16 == 8 + k) & (l16 == lane0 + 1)))
            edge += mm(pick, src, NT)
        pieces = [edge, wgt[2 * side], wgt[2 * side + 1], listing, jnp.zeros((AREA - 40, 128), F32)]
        blocks.append(jnp.concatenate(pieces, axis=0))
    area = pltpu.make_async_copy(out_ref.at[:, 0:AREA, :], out_hbm.at[:, 0:AREA, :], out_sems.at[4])
    waves = [
        pltpu.make_async_copy(
            out_ref.at[8 * g : 8 * g + 8, AREA:SLOT_ROWS, :], out_hbm.at[8 * g : 8 * g + 8, AREA:SLOT_ROWS, :], out_sems.at[g]
        )
        for g in range(4)
    ]
    for g in range(4):
        same = lax.axis_index("grp") == g
        left = jnp.where(same, blocks[0], spread)
        right = jnp.where(same, blocks[1], spread)
        for t in range(8):
            to_left = ((me_lon + 7) & 7) == t
            out_ref[g * 8 + t, 0:AREA, :] = jnp.where(to_left, left, right).astype(BF16)
    area.start()
    moved = mm(order, sums)
    low, high = moved[:320], moved[320:]
    for g in range(4):
        tile = jnp.concatenate([low[:, 64 * g : 64 * g + 64], high[:, 64 * g : 64 * g + 64]], axis=1)
        for t in range(8):
            out_ref[g * 8 + t, AREA:SLOT_ROWS, :] = tile[40 * t : 40 * t + 40].astype(BF16)
        waves[g].start()
    for c in waves + [area]:
        c.wait()


def rim_kernel(wet_hbm, diff_hbm, grid_hbm, up_ref, down_ref, wet_ref, diff_ref, rows_ref, sems):
    pairs = [(wet_hbm, wet_ref), (diff_hbm, diff_ref), (grid_hbm.at[0:2], rows_ref.at[0:2]),
             (grid_hbm.at[18:20], rows_ref.at[2:4])]
    copies = [pltpu.make_async_copy(a, b, sems.at[i]) for i, (a, b) in enumerate(pairs)]
    for c in copies:
        c.start()
    for c in copies:
        c.wait()
    row8 = iota((8, 640), 0)
    for n, (ref, first) in enumerate(((up_ref, 0), (down_ref, 18))):
        for i in range(2):
            r = first + i
            wet = wet_ref[r : r + 1, :].astype(F32)
            hi, lo = split_hi_lo(diff_ref[r : r + 1, :] * wet)
            extra = jnp.zeros((8, 640), F32)
            for m, x in enumerate((wet, hi, lo)):
                extra = jnp.where(row8 == m, x, extra)
            ref[i, 0:32, :] = rows_ref[2 * n + i]
            ref[i, 32:40, :] = extra.astype(BF16)


def remap_kernel(list_ref, recv_ref, wgt_ref, wet_ref, diff_ref,
                 rec_ref, tail_ref, planes_ref, up_ref, down_ref):
    me_grp, me_lon = lax.axis_index("grp"), lax.axis_index("lon")
    slot_l = me_grp * 8 + ((me_lon + 7) & 7)
    slot_r = me_grp * 8 + ((me_lon + 1) & 7)
    row8 = iota((8, 1), 0)

    def ids(k, s, centre):
        h = (k >= 3).astype(I32) + (k >= 6).astype(I32) + (k >= 9).astype(I32)
        lon = (centre + k - 3 * h + 7) & 7
        row = (s * 205) >> 10
        return h * 8 + lon, (s - 5 * row) * 20 + row

    lists = [tuple(upright(list_ref[c]) for c in range(3))]
    for slot in (slot_l, slot_r):
        rows = recv_ref[slot, ROW_LIST : ROW_LIST + 8, :].astype(F32).astype(I32)
        lists.append((rows[:, 0:1], rows[:, 1:2], rows[:, 2:3]))
    pairs = [ids(k, s, me_lon + shift) for (k, s, _), shift in zip(lists, (0, 7, 1))]
    slot_id = jnp.concatenate([p[0] for p in pairs], axis=0)
    block_id = jnp.concatenate([p[1] for p in pairs], axis=0)
    in_block = jnp.where(iota((24, 104), 1) == block_id, 1.0, 0.0)
    source = jnp.zeros((24, 128), F32)
    for slot in range(32):
        pick = jnp.where(slot_id == slot, in_block, 0.0).astype(BF16)
        source += mm(pick, recv_ref[slot, 0:AREA, :])
    own = source[0:8].astype(BF16)
    prod = jnp.zeros((8, 128), F32)
    for e in range(8):
        prod = jnp.where(row8 == e, mm(own, wgt_ref[e], NT), prod)
    target = lists[0][2]
    trow = (target * 205) >> 10
    place = jnp.where(iota((8, 256), 1) == (target - 5 * trow) * 32 + trow, 1.0, 0.0)
    placed = mm(place, prod, TN, lax.Precision.HIGHEST)
    received = jnp.concatenate([placed[32 * c : 32 * c + 20] for c in range(5)], axis=1)
    rec_ref[...] = received
    lane = iota((8, 128), 1)
    values, spots = [], []
    for n, (slot, lane0, col) in enumerate(((slot_l, 126, 4), (slot_r, 0, 0))):
        rows = recv_ref[slot, ROW_WGT:ROW_LIST, :].astype(F32)
        src = source[8 + 8 * n : 16 + 8 * n]
        v0 = jnp.sum(rows[0:8] * src, axis=1, keepdims=True)
        v1 = jnp.sum(rows[8:16] * src, axis=1, keepdims=True)
        values.append(jnp.where(lane == lane0, v0, 0.0) + jnp.where(lane == lane0 + 1, v1, 0.0))
        goal = lists[1 + n][2]
        grow = (goal * 205) >> 10
        spots.append(jnp.where((lane == grow) & (goal - 5 * grow == col), 1.0, 0.0))
    rec_tail = mm(jnp.concatenate(spots, axis=0), jnp.concatenate(values, axis=0), TN, lax.Precision.HIGHEST)[0:20]
    edge = jnp.concatenate(
        [recv_ref[slot_l, 0:ROW_WGT, :].astype(F32), recv_ref[slot_r, 0:ROW_WGT, :].astype(F32)], axis=0
    ).astype(BF16)
    r32, l32 = iota((32, 128), 0), iota((32, 128), 1)

    def tail_of(k):
        pick = onehot(
            ((r32 == k) & (l32 == 126)) | ((r32 == 8 + k) & (l32 == 127))
            | ((r32 == 16 + k) & (l32 == 0)) | ((r32 == 24 + k) & (l32 == 1))
        )
        return mm(edge, pick, TN)

    for k in range(5):
        tail_ref[4 * k : 4 * k + 4] = tail_of(k).reshape(4, 32, 128).astype(BF16)
    last = tail_of(5)
    own_wet = wet_ref[...].astype(F32)
    wet = jnp.concatenate([own_wet, last[0:20]], axis=1)
    dif = jnp.concatenate([diff_ref[...] * own_wet, last[32:52] + last[64:84]], axis=1)
    force = wet * jnp.concatenate([received, rec_tail], axis=1)
    planes_ref[0] = wet
    planes_ref[1] = dif
    planes_ref[2] = force
    fhi, flo = split_hi_lo(force)
    row16 = iota((16, 128), 0)
    for ref, first in ((up_ref, 0), (down_ref, 18)):
        for i in range(2):
            r = first + i
            ref[i, 0:32, :] = tail_ref[r]
            extra = jnp.zeros((16, 128), F32)
            lines = [x[r : r + 1, 128 * c : 128 * c + 128] for x in (fhi, flo) for c in range(6)]
            lines += [last[r : r + 1], last[32 + r : 33 + r], last[64 + r : 65 + r]]
            for m, x in enumerate(lines):
                extra = jnp.where(row16 == m, x, extra)
            ref[i, 32:48, :] = extra.astype(BF16)


def step_kernel(tail_ref, planes_ref, above_ref, below_ref, above2_ref, below2_ref, grid_ref,
                out_hbm, q_ref, u_ref, q1_ref, u1_ref, wet_ref, dif_ref, c_ref, res_ref, sems):
    level0 = iota((8, WIDE), 0) == 0

    def load(r, row, end, wet, dif, force):
        wet = jnp.broadcast_to(wet, (8, WIDE))
        wet_ref[r] = wet
        dif_ref[r] = jnp.broadcast_to(dif, (8, WIDE))
        cells = jnp.concatenate([row.astype(F32), end.astype(F32)], axis=1)
        for v in range(4):
            part = cells[8 * v : 8 * v + 8]
            if v == 0:
                part = jnp.where(level0, part + force, part)
            q_ref[r, 8 * v : 8 * v + 8, :] = part
            u_ref[r, 8 * v : 8 * v + 8, :] = part * wet

    for ref, ref2, base in ((above_ref, above2_ref, 0), (below_ref, below2_ref, 22)):
        for i in range(2):
            near = ref[i, 32:40, :].astype(F32)
            far = ref2[i, 32:48, :].astype(F32)
            wet = jnp.concatenate([near[0:1], far[12:13]], axis=1)
            dif = jnp.concatenate([near[1:2] + near[2:3], far[13:14] + far[14:15]], axis=1)
            force = jnp.concatenate([far[c : c + 1] + far[6 + c : 7 + c] for c in range(6)], axis=1)
            load(base + i, ref[i, 0:32, :], ref2[i, 0:32, :], wet, dif, force)
    for r in range(20):
        load(r + 2, grid_ref[r], tail_ref[r], planes_ref[0, r : r + 1, :], planes_ref[1, r : r + 1, :],
             planes_ref[2, r : r + 1, :])

    def sides(x):
        return pltpu.roll(x, 1, axis=1) + pltpu.roll(x, WIDE - 1, axis=1)

    def first(r, carry):
        dif = dif_ref[r]
        wet = wet_ref[r]
        coef = 1.0 - dif * (wet_ref[r - 1] + wet_ref[r + 1] + sides(wet))
        c_ref[r] = coef
        for v in range(4):
            lev = pl.ds(8 * v, 8)
            total = sides(u_ref[r, lev, :]) + u_ref[r - 1, lev, :] + u_ref[r + 1, lev, :]
            q = q_ref[r, lev, :] * coef + dif * total
            q1_ref[r, lev, :] = q
            u1_ref[r, lev, :] = q * wet
        return carry

    lax.fori_loop(1, 23, first, 0, unroll=2)

    def copy(r):
        return pltpu.make_async_copy(res_ref.at[r], out_hbm.at[r], sems.at[r])

    def second(r, carry):
        coef = c_ref[r]
        dif = dif_ref[r]
        for v in range(4):
            lev = pl.ds(8 * v, 8)
            total = sides(u1_ref[r, lev, :]) + u1_ref[r - 1, lev, :] + u1_ref[r + 1, lev, :]
            q = q1_ref[r, lev, :] * coef + dif * total
            res_ref[r - 2, lev, :] = q[:, 0:640]
        copy(r - 2).start()
        return carry

    lax.fori_loop(2, 22, second, 0, unroll=2)

    def finish(r, carry):
        copy(r).wait()
        return carry

    lax.fori_loop(0, 20, finish, 0)


def turn_kernel(recv_ref, out_ref):
    norm = np.float32(1.0 / math.sqrt(5120.0))
    sums = []
    for g in range(3):
        acc = recv_ref[g * 8, AREA:SLOT_ROWS, :].astype(F32)
        for t in range(1, 8):
            acc += recv_ref[g * 8 + t, AREA:SLOT_ROWS, :].astype(F32)
        sums.append(acc)
    stack = (jnp.concatenate(sums + [jnp.zeros((8, 128), F32)], axis=0) * norm).astype(BF16)
    out = jnp.zeros((256, 128), F32)
    for j2 in range(2):
        lane = iota((128, 128), 0)
        g = (lane >= 20).astype(I32) + (lane >= 40).astype(I32)
        pick = onehot((iota((128, 128), 1) == lane + 20 * g + 20 * j2) & (lane < 60))
        lined = mm(pick, stack).astype(BF16)
        rho, lam = iota((256, 128), 0), iota((256, 128), 1)
        want = ((rho >> 2) & 1) * 64 + (rho & 1) * 32 + (((rho >> 3) + FIRST_LAT) & 31)
        place = onehot((((rho >> 1) & 1) == j2) & (lam == want))
        out += mm(place, lined, NT)
    out_ref[...] = out.astype(BF16)


def legendre_kernel(waves_hbm, table_hbm, out_ref, waves_ref, table_ref, sems):
    copies = [
        pltpu.make_async_copy(table_hbm.at[pl.ds(128 * i, 128), :], table_ref.at[pl.ds(128 * i, 128), :], sems.at[i])
        for i in range(15)
    ]
    first = pltpu.make_async_copy(waves_hbm, waves_ref, sems.at[15])
    first.start()
    for c in copies:
        c.start()
    first.wait()
    lane = iota((8, 128), 1)
    waves = [waves_ref[(l - FIRST_LAT) % 32].astype(F32) for l in range(32)]
    tiles = []
    for tau in range(15):
        tile = jnp.zeros((8, 128), F32)
        for g in range(3):
            for l in range(32):
                start = g * 640 + l * 20 - 128 * tau
                if start <= -20 or start >= 128:
                    continue
                shift = (start - 20 * g) % 128
                moved = pltpu.roll(waves[l], shift, axis=1) if shift else waves[l]
                tile = jnp.where((lane >= start) & (lane < start + 20), moved, tile)
        tiles.append(tile)
    out = jnp.zeros((8, 1280), F32)
    for i in range(15):
        copies[i].wait()
        out += mm(tiles[i].astype(BF16), table_ref[128 * i : 128 * i + 128, :])
    for j in range(4):
        out_ref[j] = out[2 * j : 2 * j + 2]


VMEM = pl.BlockSpec(memory_space=pltpu.VMEM)
SMEM = pl.BlockSpec(memory_space=pltpu.SMEM)
HBM = pl.BlockSpec(memory_space=pltpu.HBM)


def call(kernel, name, smem, vmem, hbm, outs, scratch=(), out_space=VMEM, limit=None):
    flat = [jax.ShapeDtypeStruct(s, d) for s, d in outs]
    return pl.pallas_call(
        kernel,
        name=name,
        out_shape=flat if len(flat) > 1 else flat[0],
        in_specs=[SMEM] * len(smem) + [VMEM] * len(vmem) + [HBM] * len(hbm),
        out_specs=[out_space] * len(flat) if len(flat) > 1 else out_space,
        scratch_shapes=list(scratch),
        compiler_params=pltpu.CompilerParams(vmem_limit_bytes=limit and limit * 1024 * 1024),
    )(*smem, *vmem, *hbm)


def trig_tables():
    phase = np.arange(128)[:, None] * np.arange(640)[None, :] % 5120
    angle = 2.0 * np.pi / 5120.0 * phase
    return np.cos(angle).astype(np.float32), np.sin(angle).astype(np.float32)


def shards(grid_state, legendre, sent_field, wet_mask, diffusivity, remap_blocks, remap_weights):
    rows = grid_state.transpose(1, 0, 2)
    listing = remap_blocks.transpose(0, 3, 1, 2).reshape(3, 1, 8)
    weights = remap_weights[0, 0]
    bands = lax.axis_size(("grp", "lat"))
    to_before = [((i + 1) % bands, i) for i in range(bands)]
    to_after = [(i, (i + 1) % bands) for i in range(bands)]
    cos0, sin0 = trig_tables()
    packed = call(
        pack_kernel, "pack", (), (),
        (jnp.asarray(cos0), jnp.asarray(sin0), listing, rows, sent_field, wet_mask, diffusivity, weights),
        [((32, SLOT_ROWS, 128), BF16)],
        scratch=[pltpu.VMEM((32, SLOT_ROWS, 128), BF16), pltpu.VMEM((128, 640), F32), pltpu.VMEM((128, 640), F32), pltpu.VMEM((3, 1, 8), I32), pltpu.VMEM((20, 32, 640), BF16),
                 pltpu.VMEM((20, 640), F32), pltpu.VMEM((20, 640), I32), pltpu.VMEM((20, 640), F32),
                 pltpu.VMEM((2, 8, 16, 128), BF16), pltpu.SemaphoreType.DMA((9,)), pltpu.SemaphoreType.DMA((5,))],
        out_space=HBM,
    )
    plane = lax.all_to_all(packed, ("grp", "lon"), 0, 0, tiled=True)
    up, down = call(
        rim_kernel, "rim", (), (), (wet_mask, diffusivity, rows),
        [((2, 40, 640), BF16), ((2, 40, 640), BF16)],
        scratch=[pltpu.VMEM((20, 640), I32), pltpu.VMEM((20, 640), F32), pltpu.VMEM((4, 32, 640), BF16),
                 pltpu.SemaphoreType.DMA((4,))],
    )
    below = lax.ppermute(up, ("grp", "lat"), to_before)
    above = lax.ppermute(down, ("grp", "lat"), to_after)
    plane, above, below = lax.optimization_barrier((plane, above, below))
    turned = call(turn_kernel, "turn", (), (plane,), (), [((256, 128), BF16)], limit=16)
    waves = lax.all_to_all(
        turned.reshape(32, 8, 128), "lat", 0, 0, tiled=True, axis_index_groups=[[(i + FIRST_LAT) % 32 for i in range(32)]]
    )
    received, tail, planes, up2, down2 = call(
        remap_kernel, "remap", (), (listing, plane, weights, wet_mask, diffusivity), (),
        [((20, 640), F32), ((20, 32, 128), BF16), ((3, 20, WIDE), F32), ((2, 48, 128), BF16), ((2, 48, 128), BF16)],
        limit=16,
    )
    below2 = lax.ppermute(up2, ("grp", "lat"), to_before)
    above2 = lax.ppermute(down2, ("grp", "lat"), to_after)
    stepped = call(
        step_kernel, "step", (), (tail, planes, above, below, above2, below2, rows), (),
        [((20, 32, 640), F32)],
        scratch=[pltpu.VMEM((24, 32, WIDE), F32)] * 4 + [pltpu.VMEM((24, 8, WIDE), F32)] * 3
        + [pltpu.VMEM((20, 32, 640), F32), pltpu.SemaphoreType.DMA((20,))],
        out_space=HBM, limit=32,
    )
    table, stepped = lax.optimization_barrier((legendre[0], stepped))
    spectral = call(
        legendre_kernel, "legendre", (), (), (waves, table), [((4, 2, 1280), F32)],
        scratch=[pltpu.VMEM((32, 8, 128), BF16), pltpu.VMEM((1920, 1280), BF16), pltpu.SemaphoreType.DMA((16,))],
    )
    return spectral.reshape(1, 4, 2, 1280), received, stepped.transpose(1, 0, 2)


def solution(mesh):
    in_specs = (
        P(None, ("grp", "lat"), "lon"),
        P(("grp", "lat"), None, None),
        P(("grp", "lat"), "lon"),
        P(("grp", "lat"), "lon"),
        P(("grp", "lat"), "lon"),
        P(("grp", "lat"), "lon", None, None),
        P(("grp", "lat"), "lon", None, None, None),
    )
    out_specs = (
        P(("grp", "lat"), "lon", None, None),
        P(("grp", "lat"), "lon"),
        P(None, ("grp", "lat"), "lon"),
    )
    return jax.shard_map(shards, mesh=mesh, in_specs=in_specs, out_specs=out_specs, check_vma=False)
```
